128 devices in a mesh: rows: 32 (over z, x, core), rep: 4 (over y).
Axes of the slice: x: 4, y: 4, z: 4, core: 2. Of those that a mesh axis runs over, the one named last changes fastest.
Arguments:
- right_side: float32 [131072, 1024], P(('rep', 'rows')), parts along dimension 0, may hold values from -6 to 6
- leaf_inverse: float32 [131072, 1024], P(('rep', 'rows')), parts along dimension 0, may hold values from -0.1875 to 0.1875
- left_factors: float32 [5, 131072, 64], P(None, ('rep', 'rows')), parts along dimension 1, may hold values from -0.75 to 0.75
- right_factors: float32 [5, 131072, 64], P(None, ('rep', 'rows')), parts along dimension 1, may hold values from -0.21875 to 0.21875, as said below
- cores: float32 [124, 128, 128], P('rep'), parts along dimension 0, may hold values from -0.5 to 0.5
Outputs:
- solution: float32 [131072, 1024], P(('rep', 'rows')), parts along dimension 0
The draws below stay inside these ranges and needn't reach their ends.
There are 4 independent parts, one for each index of `rep`. The reference program is written for one: setup_inputs(seed, part) draws one part's arguments, and reference() takes and returns one part's arrays. A program takes and returns all parts, laid end to end along the dimension named above; each array names one. Nothing has to cross between parts.
Inputs may be any that keep to these rules, and one draw needn't show every extreme that they name: `right_factors`: level j's entries are of order (32768 / 2^(j+1))^(-1/2).
All inputs are finite; a program needn't handle non-finite values.
Results may differ from the reference program's by a relative error of at most 0.00016.
Values sent between devices are 32-bit elements; how exact they have to be, the bound alone decides.
No kernel may reach another device: no remote copies, remote signals or barrier semaphores. Data moves between devices by JAX's collectives and lax.ppermute only.
A program may use at most 128 MiB of HBM per device.

```python
import jax
import jax.numpy as jnp
from jax import lax

COLS = 1024
RANK = 64
LEVELS = 5
NTOT = 32768
LEAF = 1024
NODES = 31


def draw_right_factors(key, part):
    depth = jnp.arange(LEVELS).astype(jnp.float32)
    scale = (NTOT / 2.0 ** (depth + 1.0)) ** (-0.5)
    normal = jax.random.truncated_normal(key, -6.0, 6.0, (LEVELS, NTOT, RANK), jnp.float32)
    return normal * scale[:, None, None]


def steps_of(key, extent, cuts, smallest, largest):
    def one(dim, blocks):
        heights = jax.random.uniform(jax.random.fold_in(jax.random.fold_in(key, 6), dim), (blocks,), jnp.float32, smallest / len(cuts), largest / len(cuts))
        return jnp.repeat(jnp.exp(heights), extent[dim] // blocks).reshape((-1,) + (1,) * (len(extent) - dim - 1))

    level = one(*cuts[0])
    for cut in cuts[1:]:
        level = level * one(*cut)
    return level


def normal_values(stream_key, dims, deviation, limit, cuts=(), kind=jnp.bfloat16):
    drawn = jax.random.normal(stream_key, dims, jnp.float32) * deviation
    if len(cuts) > 0:
        drawn = steps_of(stream_key, dims, cuts, -0.22, 0.18) * drawn
    return jnp.clip(drawn, min=-limit, max=limit).astype(kind)


def setup_inputs(seed: int = 0, part: int = 0) -> dict:
    key_list = jax.random.split(jax.random.key(seed), 6)
    own_keys = jax.random.split(jax.random.fold_in(key_list[5], part), 6)
    right_side = normal_values(own_keys[0], (NTOT, COLS), 1.0, 6.0, ((0, 32),), jnp.float32)
    leaf_inverse = normal_values(own_keys[1], (NTOT, LEAF), LEAF ** -0.5, 0.1875, ((0, 32),), jnp.float32)
    left_factors = normal_values(own_keys[2], (LEVELS, NTOT, RANK), RANK ** -0.5, 0.75, ((1, 32),), jnp.float32)
    right_factors = draw_right_factors(jax.random.fold_in(jax.random.fold_in(key_list[5], part), 71), part)
    cores = normal_values(own_keys[4], (NODES, 2 * RANK, 2 * RANK), (2 * RANK) ** -0.5, 0.5, (), jnp.float32)
    return dict(right_side=right_side, leaf_inverse=leaf_inverse, left_factors=left_factors, right_factors=right_factors, cores=cores)


HIGH = lax.Precision.HIGHEST


def reference(right_side, leaf_inverse, left_factors, right_factors, cores):
    blocks = NTOT // LEAF
    solved = jnp.einsum("bij,bjk->bik", leaf_inverse.reshape(blocks, LEAF, LEAF), right_side.reshape(blocks, LEAF, COLS), precision=HIGH).reshape(NTOT, COLS)
    for level in reversed(range(LEVELS)):
        nodes = 2 ** level
        half = NTOT // nodes // 2
        shaped = solved.reshape(nodes, 2, half, COLS)
        basis_v = right_factors[level].reshape(nodes, 2, half, RANK)
        basis_u = left_factors[level].reshape(nodes, 2, half, RANK)
        projected = jnp.einsum("nchr,nchk->ncrk", basis_v, shaped, precision=HIGH)
        stacked = jnp.concatenate([projected[:, 1], projected[:, 0]], axis=1)
        core_set = cores[nodes - 1: 2 * nodes - 1]
        image = jnp.einsum("nst,ntk->nsk", core_set, stacked, precision=HIGH).reshape(nodes, 2, RANK, COLS)
        update = jnp.einsum("nchr,ncrk->nchk", basis_u, image, precision=HIGH)
        solved = (shaped - update).reshape(NTOT, COLS)
    return solved
```

```python
import jax
import jax.numpy as jnp
from jax import lax
from jax.sharding import PartitionSpec as P

PREC = lax.Precision.HIGH
R = 64


def mm(a, b):
    return jnp.dot(a, b, precision=PREC, preferred_element_type=jnp.float32)


def to_other_core(value):
    return lax.ppermute(value, "rows", [(i, i ^ 1) for i in range(32)])


def along_x(value, d):
    return lax.ppermute(value, "rows", [(i, i ^ (d << 1)) for i in range(32)])


def along_z(value, d):
    return lax.ppermute(value, "rows", [(i, i ^ (d << 3)) for i in range(32)])


def oriented(core, bit):
    return jnp.where(bit == 0, jnp.roll(core, R, axis=1), jnp.roll(core, R, axis=0))


def ordered(first, second, bit, axis):
    return jnp.where(
        bit == 0, jnp.concatenate([first, second], axis), jnp.concatenate([second, first], axis)
    )


def local(right_side, leaf_inverse, left_factors, right_factors, cores):
    me = lax.axis_index("rows")
    bit = [(me >> b) & 1 for b in range(5)]
    cols = right_side.shape[1]
    half, block = cols // 2, cols // 8
    c, x = bit[0], (me >> 1) & 3

    v = right_factors.transpose(1, 0, 2).reshape(-1, 5 * R)
    u = left_factors.transpose(1, 0, 2).reshape(-1, 5 * R)
    w = lax.dot_general(v[:, : 4 * R], u[:, R:], (((0,), (0,)), ((), ())), precision=PREC)
    w_other = to_other_core(w)
    y = lax.dot_general(v, leaf_inverse, (((0,), (0,)), ((), ())), precision=PREC)
    b_other = lax.dynamic_slice_in_dim(right_side, (1 - c) * half, half, 1)
    b_mine = lax.dynamic_slice_in_dim(right_side, c * half, half, 1)
    g_mine_t = mm(y, b_other)
    g_other = to_other_core(g_mine_t)
    g_mine = mm(y, b_mine)

    def core(i):
        return lax.dynamic_index_in_dim(cores, i, 0, keepdims=False)

    c4 = oriented(core(15 + (me >> 1)), bit[0])
    m4 = mm(jnp.concatenate([w[:, 3 * R :], w_other[:, 3 * R :]], 1), c4)
    p4 = jnp.concatenate([g_mine[4 * R :], g_other[4 * R :]], 0)
    q4 = mm(c4, p4)
    a = g_mine[: 4 * R] + g_other[: 4 * R] - mm(m4, p4)
    q4_back = to_other_core(q4[R:])
    q4_full = ordered(q4[:R], q4_back, c, 1)

    wc = w + w_other
    packed = jnp.concatenate(
        [
            wc[: 3 * R, 2 * R : 3 * R],
            jnp.concatenate([wc[: 2 * R, R : 2 * R], wc[:R, :R]], 0),
        ],
        1,
    )

    def x_message(d):
        return jnp.concatenate(
            [lax.dynamic_slice_in_dim(a, (x ^ d) * block, block, 1), packed], 0
        )

    got = [x_message(0)] + [along_x(x_message(d), d) for d in (1, 2, 3)]
    w3 = [g[4 * R :, :R] for g in got]
    w2 = [g[4 * R : 6 * R, R:] for g in got]
    w1 = sum(g[6 * R :, R:] for g in got)

    def two(c_, first, second, rows):
        return mm(c_, jnp.concatenate([first[rows : rows + R], second[rows : rows + R]], 0))

    q3, a3 = [], []
    for k in range(2):
        c3 = oriented(core(7 + ((me >> 2) ^ k)), bit[1])
        g0, g1 = got[2 * k], got[2 * k + 1]
        q = two(c3, g0, g1, 3 * R)
        q3 += [q[:R], q[R:]]
        a3.append(
            g0[: 3 * R] + g1[: 3 * R] - mm(jnp.concatenate([w3[2 * k], w3[2 * k + 1]], 1), q)
        )
    c2 = oriented(core(3 + (me >> 3)), bit[2])
    q2 = two(c2, a3[0], a3[1], 2 * R)
    t = (
        a3[0][: 2 * R]
        + a3[1][: 2 * R]
        - mm(jnp.concatenate([w2[0] + w2[1], w2[2] + w2[3]], 1), q2)
    )

    z_message = jnp.concatenate([t, jnp.concatenate([w1[: R // 2], w1[R // 2 :]], 1)], 0)
    s = [z_message] + [along_z(z_message, d) for d in (1, 2, 3)]
    w1s = [jnp.concatenate([e[2 * R :, :R], e[2 * R :, R:]], 0) for e in s]
    a1, q1 = [], []
    for k in range(2):
        c1 = oriented(core(1 + ((me >> 4) ^ k)), bit[3])
        s0, s1 = s[2 * k], s[2 * k + 1]
        q = two(c1, s0, s1, R)
        q1.append(q)
        a1.append(s0[:R] + s1[:R] - mm(jnp.concatenate([w1s[2 * k], w1s[2 * k + 1]], 1), q))
    c0 = oriented(core(0), bit[4])
    q0 = two(c0[:R], a1[0], a1[1], 0)

    def back(d):
        child = q2[:R] if d < 2 else q2[R:]
        return jnp.concatenate([q0, q1[0][:R], child, q3[d]], 0)

    r = [back(0)] + [along_x(back(d), d) for d in (1, 2, 3)]
    q_half = ordered(
        ordered(r[0], r[1], bit[1], 1), ordered(r[2], r[3], bit[1], 1), bit[2], 1
    )
    q_rest = to_other_core(q_half)
    q_all = jnp.concatenate([ordered(q_half, q_rest, c, 1), q4_full], 0)
    return mm(leaf_inverse, right_side) - mm(u, q_all)


def solution(mesh):
    in_specs = (
        P(("rep", "rows"), None),
        P(("rep", "rows"), None),
        P(None, ("rep", "rows"), None),
        P(None, ("rep", "rows"), None),
        P("rep", None, None),
    )
    out_specs = P(("rep", "rows"), None)
    return jax.shard_map(local, mesh=mesh, in_specs=in_specs, out_specs=out_specs, check_vma=False)
```

```python
import jax
import jax.numpy as jnp
from jax import lax
from jax.experimental import pallas as pl
from jax.experimental.pallas import tpu as pltpu
from jax.sharding import PartitionSpec as P

R = 64
F32, BF16 = jnp.float32, jnp.bfloat16
MIB = 1 << 20


def split(a):
    high = a.astype(BF16)
    return high, (a - high.astype(F32)).astype(BF16)


def dot(a, b, dims=((1,), (0,))):
    return lax.dot_general(a, b, (dims, ((), ())), preferred_element_type=F32)


def mm3(a, b, dims=((1,), (0,))):
    (ah, al), (bh, bl) = a, b
    return dot(ah, bh, dims) + (dot(ah, bl, dims) + dot(al, bh, dims))


def mm(a, b):
    return mm3(split(a), split(b))


def tall(ah, al, bh, bl):
    m = ah.shape[0]
    both = dot(jnp.concatenate([ah, al], 0), bh)
    return both[:m] + (both[m:] + dot(ah, bl))


def bits(me_ref):
    me = me_ref[0]
    return me, [lax.rem(me >> b, 2) for b in range(5)]


VM = pl.BlockSpec(memory_space=pltpu.VMEM)
SM = pl.BlockSpec(memory_space=pltpu.SMEM)
HB = pl.BlockSpec(memory_space=pltpu.HBM)


def shape(*dims, dtype=F32):
    return jax.ShapeDtypeStruct(dims, dtype)


def call(kernel, ins, outs, specs, name, flops, moved, limit, scratch=(), grid=None, aliases=None):
    out_specs = [VM] * len(outs) if grid is None else grid[1]
    extra = {} if grid is None else dict(grid=grid[0])
    return pl.pallas_call(
        kernel,
        out_shape=tuple(outs),
        in_specs=specs,
        out_specs=tuple(out_specs),
        scratch_shapes=list(scratch),
        name=name,
        input_output_aliases=aliases or {},
        cost_estimate=pl.CostEstimate(flops=flops, bytes_accessed=moved, transcendentals=0),
        compiler_params=pltpu.CompilerParams(vmem_limit_bytes=limit * MIB),
        **extra,
    )(*ins)


CH = 4


def k1(me_ref, vt_hbm, ut_hbm, l_hbm, b_hbm, cores_hbm, msg, yh_ref, yl_ref, sel, vt, ut, l, b, sems):
    me, bit = bits(me_ref)
    n = l.shape[1] // CH
    half = b.shape[1]
    where = [15 + (me >> 1), 7 + (me >> 2), 7 + ((me >> 2) ^ 1), 3 + (me >> 3), 1 + (me >> 4), 1 + ((me >> 4) ^ 1), 0]
    start = pl.multiple_of((1 - bit[0]) * half, half)

    def col(k):
        return pl.ds(k * n, n)

    copies = [pltpu.make_async_copy(vt_hbm, vt, sems.at[0])]
    copies += [
        pltpu.make_async_copy(l_hbm.at[:, col(k)], l.at[:, col(k)], sems.at[1 + k]) for k in range(CH)
    ]
    copies += [pltpu.make_async_copy(ut_hbm, ut, sems.at[1 + CH])]
    copies += [
        pltpu.make_async_copy(
            b_hbm.at[:, pl.ds(pl.multiple_of(start + k * n, n), n)], b.at[:, col(k)], sems.at[2 + CH + k]
        )
        for k in range(half // n)
    ]
    picks = [
        pltpu.make_async_copy(cores_hbm.at[i], sel.at[k], sems.at[10 + k]) for k, i in enumerate(where)
    ]
    for copy in copies + picks:
        copy.start()
    copies[0].wait()
    vh, vl = split(vt[...])
    for k in range(CH):
        copies[1 + k].wait()
        lh, ll = split(l[:, k * n : k * n + n])
        y = tall(vh, vl, lh, ll)
        yh, yl = split(y)
        yh_ref[:, k * n : k * n + n] = yh
        yl_ref[:, k * n : k * n + n] = yl
    copies[1 + CH].wait()
    uh, ul = split(ut[R:, :])
    w = mm3((vh[: 4 * R], vl[: 4 * R]), (uh, ul), ((1,), (1,)))
    msg[5 * R :, : 4 * R] = w[: 2 * R]
    msg[5 * R :, 4 * R :] = w[2 * R :]
    for k in range(half // n):
        copies[2 + CH + k].wait()
        bh, bl = split(b[:, k * n : k * n + n])
        msg[: 5 * R, k * n : k * n + n] = tall(yh_ref[...], yl_ref[...], bh, bl)
    for copy in picks:
        copy.wait()


def k2(me_ref, yh, yl, b_hbm, g, b, sems):
    me, bit = bits(me_ref)
    half = b.shape[1]
    n = half // 2
    start = pl.multiple_of(bit[0] * half, half)
    copies = [
        pltpu.make_async_copy(
            b_hbm.at[:, pl.ds(pl.multiple_of(start + k * n, n), n)], b.at[:, pl.ds(k * n, n)], sems.at[k]
        )
        for k in range(2)
    ]
    for copy in copies:
        copy.start()
    for k in range(2):
        copies[k].wait()
        bh, bl = split(b[:, k * n : k * n + n])
        g[:, k * n : k * n + n] = tall(yh[...], yl[...], bh, bl)


def k3(me_ref, g, own, got, sel, m0, m1, m2, m3, q_mine, q_other, p, q):
    me, bit = bits(me_ref)
    x = lax.rem(me >> 1, 4)
    c = bit[0]
    p[pl.ds(pl.multiple_of((1 - c) * R, R), R), :] = g[4 * R :, :]
    p[pl.ds(pl.multiple_of(c * R, R), R), :] = got[4 * R : 5 * R, :]
    q[...] = mm(sel[0], p[...])
    q_mine[...] = q[pl.ds(pl.multiple_of(c * R, R), R), :]
    q_other[...] = q[pl.ds(pl.multiple_of((1 - c) * R, R), R), :]

    def level(ref, j, rows):
        if rows <= 2:
            return ref[5 * R : (5 + rows) * R, (j - 1) * R : j * R]
        low = ref[5 * R :, (j - 1) * R : j * R]
        high = ref[5 * R : (3 + rows) * R, (j + 3) * R : (j + 4) * R]
        return jnp.concatenate([low, high], 0)

    wide = split(jnp.concatenate([level(own, 4, 4), level(got, 4, 4)], 1))
    third = level(own, 3, 3) + level(got, 3, 3)
    second = level(own, 2, 2) + level(got, 2, 2)
    first = level(own, 1, 1) + level(got, 1, 1)
    packed = jnp.concatenate([third, jnp.concatenate([second, first], 0)], 1)
    for d, out in ((2, m2), (1, m1), (3, m3), (0, m0)):
        at = pl.ds(pl.multiple_of((x ^ d) * 2 * R, 2 * R), 2 * R)
        both = split(jnp.concatenate([q_mine[:, at], q_other[:, at]], 0))
        out[: 4 * R, :] = g[: 4 * R, at] + got[: 4 * R, at] - mm3(wide, both)
        out[4 * R :, :] = packed


def pair(p, core, first, second, bit):
    p[pl.ds(pl.multiple_of((1 - bit) * R, R), R), :] = first
    p[pl.ds(pl.multiple_of(bit * R, R), R), :] = second
    return mm(core, p[...])


def rows_of(q, bit, own):
    at = bit if own else 1 - bit
    return q[pl.ds(pl.multiple_of(at * R, R), R), :]


def k4(me_ref, g0, g2, g1, g3, sel, z, q3, q2, p, q):
    me, bit = bits(me_ref)
    got = (g0, g1, g2, g3)
    sums = []
    for k in range(2):
        a, b = got[2 * k], got[2 * k + 1]
        q.at[k][...] = pair(p.at[k], sel[1 + k], a[3 * R : 4 * R, :], b[3 * R : 4 * R, :], bit[1])
    for k in range(2):
        a, b = got[2 * k], got[2 * k + 1]
        mine, theirs = rows_of(q.at[k], bit[1], True), rows_of(q.at[k], bit[1], False)
        q3[2 * k] = mine
        q3[2 * k + 1] = theirs
        w = jnp.concatenate([a[4 * R :, :R], b[4 * R :, :R]], 1)
        sums.append(a[: 3 * R, :] + b[: 3 * R, :] - mm(w, jnp.concatenate([mine, theirs], 0)))
    q.at[2][...] = pair(p.at[2], sel[3], sums[0][2 * R :], sums[1][2 * R :], bit[2])
    mine, theirs = rows_of(q.at[2], bit[2], True), rows_of(q.at[2], bit[2], False)
    q2[0] = mine
    q2[1] = theirs
    w = jnp.concatenate(
        [
            g0[4 * R : 6 * R, R:] + g1[4 * R : 6 * R, R:],
            g2[4 * R : 6 * R, R:] + g3[4 * R : 6 * R, R:],
        ],
        1,
    )
    z[: 2 * R, :] = sums[0][: 2 * R] + sums[1][: 2 * R] - mm(w, jnp.concatenate([mine, theirs], 0))
    z[2 * R :, :] = (g0[6 * R :, :] + g1[6 * R :, :]) + (g2[6 * R :, :] + g3[6 * R :, :])


def k5(me_ref, s0, s3, s1, s2, sel, q3, q2, r0, r1, r2, r3, p, q):
    me, bit = bits(me_ref)
    s = (s0, s1, s2, s3)
    sums = []
    for k in range(2):
        a, b = s[2 * k], s[2 * k + 1]
        q.at[k][...] = pair(p.at[k], sel[4 + k], a[R : 2 * R, :], b[R : 2 * R, :], bit[3])
    for k in range(2):
        a, b = s[2 * k], s[2 * k + 1]
        both = jnp.concatenate([rows_of(q.at[k], bit[3], True), rows_of(q.at[k], bit[3], False)], 0)
        w = jnp.concatenate([a[2 * R :, R:], b[2 * R :, R:]], 1)
        sums.append(a[:R, :] + b[:R, :] - mm(w, both))
    q.at[2][...] = pair(p.at[2], sel[6], sums[0], sums[1], bit[4])
    top = rows_of(q.at[2], bit[4], True)
    one = rows_of(q.at[0], bit[3], True)
    for d, out in ((2, r2), (1, r1), (3, r3), (0, r0)):
        out[:R, :] = top
        out[R : 2 * R, :] = one
        out[2 * R : 3 * R, :] = q2[d // 2]
        out[3 * R :, :] = q3[d]


def k6(me_ref, r0, r2, r1, r3, q_half):
    me, bit = bits(me_ref)
    x = lax.rem(me >> 1, 4)
    for d, r in ((0, r0), (1, r1), (2, r2), (3, r3)):
        q_half[:, pl.ds(pl.multiple_of((x ^ d) * 2 * R, 2 * R), 2 * R)] = r[...]


def ku(ut, uh_ref, ul_ref):
    uh_ref[...], ul_ref[...] = split(ut[...].T)


def kl(l, b, uh, ul, q4, x):
    x[...] = mm(l[...], b[...]) - mm3((uh[:, 4 * R :], ul[:, 4 * R :]), split(q4[...]))


def k7(x, uh, ul, q, *rest):
    rest[-1][...] = x[...] - mm3((uh[:, : 4 * R], ul[:, : 4 * R]), split(q[...]))


def to_other_core(value):
    return lax.ppermute(value, "rows", [(i, i ^ 1) for i in range(32)])


def along(value, shift, d):
    return lax.ppermute(value, "rows", [(i, i ^ (d << shift)) for i in range(32)])


def spread(values, shift, order=(0, 2, 1, 3)):
    got = {0: values[0]}
    for d in (2, 1, 3):
        got[d] = along(values[d], shift, d)
    return [got[d] for d in order]


def local(right_side, leaf_inverse, left_factors, right_factors, cores):
    me = lax.axis_index("rows").astype(jnp.int32).reshape(1)
    rows, cols = right_side.shape
    half, eighth = cols // 2, cols // 8
    vt = right_factors.transpose(0, 2, 1).reshape(5 * R, rows)
    ut = left_factors.transpose(0, 2, 1).reshape(5 * R, rows)
    n = cols // CH
    in_hbm = [pltpu.with_memory_space_constraint(v, pltpu.HBM) for v in (vt, ut, leaf_inverse, right_side, cores)]

    msg, yh, yl, sel = call(
        k1, (me, *in_hbm),
        [shape(7 * R, half), shape(5 * R, rows, dtype=BF16), shape(5 * R, rows, dtype=BF16), shape(7, 2 * R, 2 * R)],
        [SM, HB, HB, HB, HB, HB], "project", 7 * 10**9, 9 * MIB, 20,
        scratch=[
            pltpu.VMEM((5 * R, rows), F32), pltpu.VMEM((5 * R, rows), F32), pltpu.VMEM((rows, cols), F32),
            pltpu.VMEM((rows, half), F32), pltpu.SemaphoreType.DMA((20,)),
        ],
    )
    got = to_other_core(msg)
    (g,) = call(
        k2, (me, yh, yl, in_hbm[3]), [shape(5 * R, half)], [SM, VM, VM, HB], "project_own",
        2 * 10**9, 3 * MIB, 10, scratch=[pltpu.VMEM((rows, half), F32), pltpu.SemaphoreType.DMA((2,))],
    )
    c = me[0] & 1
    uh, ul = call(
        ku, (lax.optimization_barrier((ut, g))[0],), [shape(rows, 5 * R, dtype=BF16)] * 2, [VM], "turn", 10, 3 * MIB, 8,
    )
    tile = 256

    def leaf(which, q4):
        def at(i, s):
            return (0, s[0])

        return pl.pallas_call(
            lambda s, l, b, u1, u2, q, x: kl(l, b, u1, u2, q, x),
            out_shape=shape(rows, half),
            grid_spec=pltpu.PrefetchScalarGridSpec(
                num_scalar_prefetch=1,
                grid=(rows // tile,),
                in_specs=[
                    pl.BlockSpec((tile, rows), lambda i, s: (i, 0)),
                    pl.BlockSpec((rows, half), at),
                    pl.BlockSpec((tile, 5 * R), lambda i, s: (i, 0)),
                    pl.BlockSpec((tile, 5 * R), lambda i, s: (i, 0)),
                    pl.BlockSpec((R, half), lambda i, s: (0, 0)),
                ],
                out_specs=pl.BlockSpec((tile, half), lambda i, s: (i, 0)),
            ),
            name="leaf",
            cost_estimate=pl.CostEstimate(flops=4 * 10**9, bytes_accessed=8 * MIB, transcendentals=0),
            compiler_params=pltpu.CompilerParams(vmem_limit_bytes=14 * MIB),
        )(which.reshape(1), leaf_inverse, right_side, uh, ul, q4)

    *messages, q4_mine, q4_other = call(
        k3, (me, g, msg, got, sel), [shape(7 * R, eighth)] * 4 + [shape(R, half)] * 2,
        [SM] + [VM] * 4, "level4", 10**9, 4 * MIB, 10,
        scratch=[pltpu.VMEM((2 * R, half), F32)] * 2,
    )
    q4_back = to_other_core(q4_other)
    small = [pltpu.VMEM((3, 2 * R, eighth), F32)] * 2
    got, x_mine = lax.optimization_barrier((spread(messages, 1), leaf(c, q4_mine)))
    z, q3, q2 = call(
        k4, (me, *got, sel),
        [shape(3 * R, eighth), shape(4, R, eighth), shape(2, R, eighth)],
        [SM] + [VM] * 5, "levels32", 10**8, MIB, 8, scratch=small,
    )
    got, x_other = lax.optimization_barrier((spread([z] * 4, 3, (0, 3, 1, 2)), leaf(1 - c, q4_back)))
    back = call(
        k5, (me, *got, sel, q3, q2), [shape(4 * R, eighth)] * 4,
        [SM] + [VM] * 7, "levels10", 10**8, MIB, 8, scratch=small,
    )
    (q_half,) = call(
        k6, (me, *spread(back, 1)), [shape(4 * R, half)], [SM] + [VM] * 4, "assemble", 10, MIB, 8,
    )
    q_rest = to_other_core(q_half)

    def finish(which, x, q, so_far):
        extra = () if so_far is None else (so_far,)
        return pl.pallas_call(
            lambda s, *refs: k7(*refs),
            out_shape=shape(rows, cols),
            grid_spec=pltpu.PrefetchScalarGridSpec(
                num_scalar_prefetch=1,
                grid=(rows // tile,),
                in_specs=[
                    pl.BlockSpec((tile, half), lambda i, s: (i, 0)),
                    pl.BlockSpec((tile, 5 * R), lambda i, s: (i, 0)),
                    pl.BlockSpec((tile, 5 * R), lambda i, s: (i, 0)),
                    pl.BlockSpec((4 * R, half), lambda i, s: (0, 0)),
                ] + [HB] * len(extra),
                out_specs=pl.BlockSpec((tile, half), lambda i, s: (i, s[0])),
            ),
            name="finish",
            input_output_aliases={5: 0} if extra else {},
            cost_estimate=pl.CostEstimate(flops=10**9, bytes_accessed=5 * MIB, transcendentals=0),
            compiler_params=pltpu.CompilerParams(vmem_limit_bytes=12 * MIB),
        )(which.reshape(1), x, uh, ul, q, *extra)

    out = finish(c, x_mine, q_half, None)
    return finish(1 - c, x_other, q_rest, out)


def solution(mesh):
    in_specs = (
        P(("rep", "rows"), None),
        P(("rep", "rows"), None),
        P(None, ("rep", "rows"), None),
        P(None, ("rep", "rows"), None),
        P("rep", None, None),
    )
    out_specs = P(("rep", "rows"), None)
    return jax.shard_map(local, mesh=mesh, in_specs=in_specs, out_specs=out_specs, check_vma=False)
```

```python
import jax
import jax.numpy as jnp
from jax import lax
from jax.experimental import pallas as pl
from jax.experimental.pallas import tpu as pltpu
from jax.sharding import PartitionSpec as P

R = 64
F32, BF16 = jnp.float32, jnp.bfloat16
MIB = 1 << 20


def split(a):
    high = a.astype(BF16)
    return high, (a - high.astype(F32)).astype(BF16)


def dot(a, b, dims=((1,), (0,))):
    return lax.dot_general(a, b, (dims, ((), ())), preferred_element_type=F32)


def mm3(a, b):
    (ah, al), (bh, bl) = a, b
    return dot(jnp.concatenate([ah, al, ah], 1), jnp.concatenate([bh, bh, bl], 0))


def mm(a, b):
    return mm3(split(a), split(b))


def bits(me_ref):
    me = me_ref[0]
    return me, [lax.rem(me >> b, 2) for b in range(5)]


VM = pl.BlockSpec(memory_space=pltpu.VMEM)
SM = pl.BlockSpec(memory_space=pltpu.SMEM)
HB = pl.BlockSpec(memory_space=pltpu.HBM)


def shape(*dims, dtype=F32):
    return jax.ShapeDtypeStruct(dims, dtype)


def call(kernel, ins, outs, specs, name, flops, moved, limit, scratch=(), grid=None, aliases=None):
    out_specs = [VM] * len(outs) if grid is None else grid[1]
    extra = {} if grid is None else dict(grid=grid[0])
    return pl.pallas_call(
        kernel,
        out_shape=tuple(outs),
        in_specs=specs,
        out_specs=tuple(out_specs),
        scratch_shapes=list(scratch),
        name=name,
        input_output_aliases=aliases or {},
        cost_estimate=pl.CostEstimate(flops=flops, bytes_accessed=moved, transcendentals=0),
        compiler_params=pltpu.CompilerParams(vmem_limit_bytes=limit * MIB),
        **extra,
    )(*ins)


CH = 4


def k1(me_ref, vt_hbm, ut_hbm, l_hbm, b_hbm, cores_hbm, msg, yh_ref, yl_ref, lh_ref, ll_ref, b, sel, vt, ut, l, sems):
    me, bit = bits(me_ref)
    n = l.shape[0] // CH
    half = b.shape[2]
    where = [15 + (me >> 1), 7 + (me >> 2), 7 + ((me >> 2) ^ 1), 3 + (me >> 3), 1 + (me >> 4), 1 + ((me >> 4) ^ 1), 0]
    rows = [pl.ds(k * n, n) for k in range(CH)]
    get_v = pltpu.make_async_copy(vt_hbm, vt, sems.at[0])
    get_l = [pltpu.make_async_copy(l_hbm.at[rows[k]], l.at[rows[k]], sems.at[1 + k]) for k in range(CH)]
    get_u = pltpu.make_async_copy(ut_hbm, ut, sems.at[1 + CH])
    get_b = [
        pltpu.make_async_copy(
            b_hbm.at[:, pl.ds(pl.multiple_of(at * half, half), half)], b.at[k], sems.at[2 + CH + k]
        )
        for k, at in enumerate((bit[0], 1 - bit[0]))
    ]
    picks = [pltpu.make_async_copy(cores_hbm.at[i], sel.at[k], sems.at[10 + k]) for k, i in enumerate(where)]
    for copy in [get_v, *get_l, get_b[1], get_u, *picks, get_b[0]]:
        copy.start()
    get_v.wait()
    vh, vl = split(vt[...])
    y = None
    for k in range(CH):
        get_l[k].wait()
        at = slice(k * n, k * n + n)
        lh, ll = split(l[at, :])
        lh_ref[at, :] = lh
        ll_ref[at, :] = ll
        part = mm3((vh[:, at], vl[:, at]), (lh, ll))
        y = part if y is None else y + part
    yh, yl = split(y)
    yh_ref[...] = yh
    yl_ref[...] = yl
    get_b[1].wait()
    msg[: 5 * R, :] = mm3((yh, yl), split(b[1]))
    get_u.wait()
    uh, ul = split(ut[R:, :])
    vh, vl = vh[: 4 * R], vl[: 4 * R]
    w = dot(jnp.concatenate([vh, vl, vh], 1), jnp.concatenate([uh, uh, ul], 1), ((1,), (1,)))
    msg[5 * R :, : 4 * R] = w[: 2 * R]
    msg[5 * R :, 4 * R :] = w[2 * R :]
    for copy in picks + [get_b[0]]:
        copy.wait()


def k2(yh, yl, b, g):
    g[...] = mm3((yh[...], yl[...]), split(b[0]))


def k3(me_ref, g, own, got, sel, m0, m1, m2, m3, q_mine, q_other, p, q):
    me, bit = bits(me_ref)
    x = lax.rem(me >> 1, 4)
    c = bit[0]
    p[pl.ds(pl.multiple_of((1 - c) * R, R), R), :] = g[4 * R :, :]
    p[pl.ds(pl.multiple_of(c * R, R), R), :] = got[4 * R : 5 * R, :]
    q[...] = mm(sel[0], p[...])
    q_mine[...] = q[pl.ds(pl.multiple_of(c * R, R), R), :]
    q_other[...] = q[pl.ds(pl.multiple_of((1 - c) * R, R), R), :]

    def level(ref, j, rows):
        if rows <= 2:
            return ref[5 * R : (5 + rows) * R, (j - 1) * R : j * R]
        low = ref[5 * R :, (j - 1) * R : j * R]
        high = ref[5 * R : (3 + rows) * R, (j + 3) * R : (j + 4) * R]
        return jnp.concatenate([low, high], 0)

    wide = split(jnp.concatenate([level(own, 4, 4), level(got, 4, 4)], 1))
    third = level(own, 3, 3) + level(got, 3, 3)
    second = level(own, 2, 2) + level(got, 2, 2)
    first = level(own, 1, 1) + level(got, 1, 1)
    packed = jnp.concatenate([third, jnp.concatenate([second, first], 0)], 1)
    for d, out in ((2, m2), (1, m1), (3, m3), (0, m0)):
        at = pl.ds(pl.multiple_of((x ^ d) * 2 * R, 2 * R), 2 * R)
        both = split(jnp.concatenate([q_mine[:, at], q_other[:, at]], 0))
        out[: 4 * R, :] = g[: 4 * R, at] + got[: 4 * R, at] - mm3(wide, both)
        out[4 * R :, :] = packed


def pair(p, core, first, second, bit):
    p[pl.ds(pl.multiple_of((1 - bit) * R, R), R), :] = first
    p[pl.ds(pl.multiple_of(bit * R, R), R), :] = second
    return mm(core, p[...])


def rows_of(q, bit, own):
    at = bit if own else 1 - bit
    return q[pl.ds(pl.multiple_of(at * R, R), R), :]


def k4(me_ref, g0, g2, g1, g3, sel, z, q3, q2, p, q):
    me, bit = bits(me_ref)
    got = (g0, g1, g2, g3)
    sums = []
    for k in range(2):
        a, b = got[2 * k], got[2 * k + 1]
        q.at[k][...] = pair(p.at[k], sel[1 + k], a[3 * R : 4 * R, :], b[3 * R : 4 * R, :], bit[1])
    for k in range(2):
        a, b = got[2 * k], got[2 * k + 1]
        mine, theirs = rows_of(q.at[k], bit[1], True), rows_of(q.at[k], bit[1], False)
        q3[2 * k] = mine
        q3[2 * k + 1] = theirs
        w = jnp.concatenate([a[4 * R :, :R], b[4 * R :, :R]], 1)
        sums.append(a[: 3 * R, :] + b[: 3 * R, :] - mm(w, jnp.concatenate([mine, theirs], 0)))
    q.at[2][...] = pair(p.at[2], sel[3], sums[0][2 * R :], sums[1][2 * R :], bit[2])
    mine, theirs = rows_of(q.at[2], bit[2], True), rows_of(q.at[2], bit[2], False)
    q2[0] = mine
    q2[1] = theirs
    w = jnp.concatenate(
        [
            g0[4 * R : 6 * R, R:] + g1[4 * R : 6 * R, R:],
            g2[4 * R : 6 * R, R:] + g3[4 * R : 6 * R, R:],
        ],
        1,
    )
    z[: 2 * R, :] = sums[0][: 2 * R] + sums[1][: 2 * R] - mm(w, jnp.concatenate([mine, theirs], 0))
    z[2 * R :, :] = (g0[6 * R :, :] + g1[6 * R :, :]) + (g2[6 * R :, :] + g3[6 * R :, :])


def k5(me_ref, s0, s2, s1, s3, sel, q3, q2, r0, r1, r2, r3, p, q):
    me, bit = bits(me_ref)
    s = (s0, s1, s2, s3)
    sums = []
    for k in range(2):
        a, b = s[2 * k], s[2 * k + 1]
        q.at[k][...] = pair(p.at[k], sel[4 + k], a[R : 2 * R, :], b[R : 2 * R, :], bit[3])
    for k in range(2):
        a, b = s[2 * k], s[2 * k + 1]
        both = jnp.concatenate([rows_of(q.at[k], bit[3], True), rows_of(q.at[k], bit[3], False)], 0)
        w = jnp.concatenate([a[2 * R :, R:], b[2 * R :, R:]], 1)
        sums.append(a[:R, :] + b[:R, :] - mm(w, both))
    q.at[2][...] = pair(p.at[2], sel[6], sums[0], sums[1], bit[4])
    top = rows_of(q.at[2], bit[4], True)
    one = rows_of(q.at[0], bit[3], True)
    for d, out in ((2, r2), (1, r1), (3, r3), (0, r0)):
        out[:R, :] = top
        out[R : 2 * R, :] = one
        out[2 * R : 3 * R, :] = q2[d // 2]
        out[3 * R :, :] = q3[d]


def k6(me_ref, r0, r2, r1, r3, q_half):
    me, bit = bits(me_ref)
    x = lax.rem(me >> 1, 4)
    for d, r in ((0, r0), (1, r1), (2, r2), (3, r3)):
        q_half[:, pl.ds(pl.multiple_of((x ^ d) * 2 * R, 2 * R), 2 * R)] = r[...]


def ku(ut, uh_ref, ul_ref):
    uh_ref[...], ul_ref[...] = split(ut[...].T)


def kl(piece, lh, ll, b, uh, ul, q4, x):
    n = x.shape[1]
    at = slice(piece % 2 * n, piece % 2 * n + n)
    bh, bl = split(b[piece // 2, :, at])
    qh, ql = split(q4[:, at])
    right = jnp.concatenate([bh, bh, bl], 0)
    below = jnp.concatenate([qh, qh, ql], 0)
    for k in range(4):
        r = slice(k * 2 * 128, (k + 1) * 2 * 128)
        u4h, u4l = uh[r, 4 * R :], ul[r, 4 * R :]
        x[r, :] = dot(jnp.concatenate([lh[r, :], ll[r, :], lh[r, :]], 1), right) - dot(
            jnp.concatenate([u4h, u4l, u4h], 1), below
        )


def k7(mine, me_ref, xa, xb, uh, ul, q, *rest):
    out, buf, sems = rest[-3:]
    me, bit = bits(me_ref)
    half = q.shape[1]
    at = pl.multiple_of((bit[0] if mine else 1 - bit[0]) * half, half)
    qh, ql = split(q[...])
    right = jnp.concatenate([qh, qh, ql], 0)
    copies = []
    for k in range(4):
        r = slice(k * 256, k * 256 + 256)
        u3h, u3l = uh[r, : 4 * R], ul[r, : 4 * R]
        buf[r, :] = jnp.concatenate([xa[r, :], xb[r, :]], 1) - dot(jnp.concatenate([u3h, u3l, u3h], 1), right)
        copies.append(
            pltpu.make_async_copy(
                buf.at[pl.ds(k * 256, 256)], out.at[pl.ds(k * 256, 256), pl.ds(at, half)], sems.at[k]
            )
        )
        copies[-1].start()
    for copy in copies:
        copy.wait()


def to_other_core(value):
    return lax.ppermute(value, "rows", [(i, i ^ 1) for i in range(32)])


def along(value, shift, d):
    return lax.ppermute(value, "rows", [(i, i ^ (d << shift)) for i in range(32)])


def spread(values, shift, order=(0, 2, 1, 3)):
    got = {0: values[0]}
    for d in (2, 1, 3):
        got[d] = along(values[d], shift, d)
    return [got[d] for d in order]


def local(right_side, leaf_inverse, left_factors, right_factors, cores):
    me = lax.axis_index("rows").astype(jnp.int32).reshape(1)
    rows, cols = right_side.shape
    half, eighth = cols // 2, cols // 8
    vt = right_factors.transpose(0, 2, 1).reshape(5 * R, rows)
    ut = left_factors.transpose(0, 2, 1).reshape(5 * R, rows)
    in_hbm = [pltpu.with_memory_space_constraint(v, pltpu.HBM) for v in (vt, ut, leaf_inverse, right_side, cores)]

    def pieces(dims, *more):
        return [shape(*dims, **kw) for kw in more]

    half_type = dict(dtype=BF16)
    msg, yh, yl, lh, ll, b, sel = call(
        k1, (me, *in_hbm),
        [shape(7 * R, half), *pieces((5 * R, rows), half_type, half_type), *pieces((rows, rows), half_type, half_type),
         shape(2, rows, half), shape(7, 2 * R, 2 * R)],
        [SM, HB, HB, HB, HB, HB], "project", 7 * 10**9, 9 * MIB, 28,
        scratch=[
            pltpu.VMEM((5 * R, rows), F32), pltpu.VMEM((5 * R, rows), F32), pltpu.VMEM((rows, rows), F32),
            pltpu.SemaphoreType.DMA((20,)),
        ],
    )
    got = to_other_core(msg)
    (g,) = call(k2, (yh, yl, b), [shape(5 * R, half)], [VM, VM, VM], "project_own", 2 * 10**9, 3 * MIB, 10)
    uh, ul = call(
        ku, (lax.optimization_barrier((ut, g))[0],), [shape(rows, 5 * R, dtype=BF16)] * 2, [VM], "turn", 10, 3 * MIB, 8,
    )

    def leaf(piece, q4):
        return call(
            lambda *refs: kl(piece, *refs), (lh, ll, b, uh, ul, q4), [shape(rows, half // 2)], [VM] * 6, "leaf",
            2 * 10**9, 6 * MIB, 12,
        )[0]

    *messages, q4_mine, q4_other = call(
        k3, (me, g, msg, got, sel), [shape(7 * R, eighth)] * 4 + [shape(R, half)] * 2,
        [SM] + [VM] * 4, "level4", 10**9, 4 * MIB, 10,
        scratch=[pltpu.VMEM((2 * R, half), F32)] * 2,
    )
    q4_back = to_other_core(q4_other)
    small = [pltpu.VMEM((3, 2 * R, eighth), F32)] * 2
    got, x0 = lax.optimization_barrier((spread(messages, 1), leaf(0, q4_mine)))
    z, q3, q2 = call(
        k4, (me, *got, sel),
        [shape(3 * R, eighth), shape(4, R, eighth), shape(2, R, eighth)],
        [SM] + [VM] * 5, "levels32", 10**8, MIB, 8, scratch=small,
    )
    got, x1 = lax.optimization_barrier((spread([z] * 4, 3), leaf(1, q4_mine)))
    back = call(
        k5, (me, *got, sel, q3, q2), [shape(4 * R, eighth)] * 4,
        [SM] + [VM] * 7, "levels10", 10**8, MIB, 8, scratch=small,
    )
    got, x2, x3 = lax.optimization_barrier((spread(back, 1), leaf(2, q4_back), leaf(3, q4_back)))
    (q_half,) = call(k6, (me, *got), [shape(4 * R, half)], [SM] + [VM] * 4, "assemble", 10, MIB, 8)
    q_rest = to_other_core(q_half)

    def finish(mine, xa, xb, q, *so_far):
        return pl.pallas_call(
            lambda *refs: k7(mine, *refs),
            out_shape=shape(rows, cols),
            in_specs=[SM] + [VM] * 5 + [HB] * len(so_far),
            out_specs=HB,
            scratch_shapes=[pltpu.VMEM((rows, half), F32), pltpu.SemaphoreType.DMA((4,))],
            name="finish",
            input_output_aliases={6: 0} if so_far else {},
            cost_estimate=pl.CostEstimate(flops=10**9, bytes_accessed=5 * MIB, transcendentals=0),
            compiler_params=pltpu.CompilerParams(vmem_limit_bytes=10 * MIB),
        )(me, xa, xb, uh, ul, q, *so_far)

    out = finish(True, x0, x1, q_half)
    return finish(False, x2, x3, q_rest, out)


def solution(mesh):
    in_specs = (
        P(("rep", "rows"), None),
        P(("rep", "rows"), None),
        P(None, ("rep", "rows"), None),
        P(None, ("rep", "rows"), None),
        P("rep", None, None),
    )
    out_specs = P(("rep", "rows"), None)
    return jax.shard_map(local, mesh=mesh, in_specs=in_specs, out_specs=out_specs, check_vma=False)
```

```python
import jax
import jax.numpy as jnp
from jax import lax
from jax.experimental import pallas as pl
from jax.experimental.pallas import tpu as pltpu
from jax.sharding import PartitionSpec as P

R = 64
F32, BF16 = jnp.float32, jnp.bfloat16
MIB = 1 << 20


def split(a):
    high = a.astype(BF16)
    return high, (a - high.astype(F32)).astype(BF16)


def dot(a, b, dims=((1,), (0,))):
    return lax.dot_general(a, b, (dims, ((), ())), preferred_element_type=F32)


def mm3(a, b):
    (ah, al), (bh, bl) = a, b
    return dot(jnp.concatenate([ah, al, ah], 1), jnp.concatenate([bh, bh, bl], 0))


def mm(a, b):
    return mm3(split(a), split(b))


def bits(me_ref):
    me = me_ref[0]
    return me, [lax.rem(me >> b, 2) for b in range(5)]


VM = pl.BlockSpec(memory_space=pltpu.VMEM)
SM = pl.BlockSpec(memory_space=pltpu.SMEM)
HB = pl.BlockSpec(memory_space=pltpu.HBM)


def shape(*dims, dtype=F32):
    return jax.ShapeDtypeStruct(dims, dtype)


def call(kernel, ins, outs, specs, name, flops, moved, limit, scratch=(), grid=None, aliases=None):
    out_specs = [VM] * len(outs) if grid is None else grid[1]
    extra = {} if grid is None else dict(grid=grid[0])
    return pl.pallas_call(
        kernel,
        out_shape=tuple(outs),
        in_specs=specs,
        out_specs=tuple(out_specs),
        scratch_shapes=list(scratch),
        name=name,
        input_output_aliases=aliases or {},
        cost_estimate=pl.CostEstimate(flops=flops, bytes_accessed=1000, transcendentals=0),
        compiler_params=pltpu.CompilerParams(vmem_limit_bytes=limit * MIB),
        **extra,
    )(*ins)


def pack(w):
    low = jnp.concatenate([w[: 2 * R, R : 2 * R], w[:R, :R]], 0)
    return jnp.concatenate([w[: 3 * R, 2 * R : 3 * R], low], 1)


def k0(me_ref, vt_hbm, ut_hbm, cores_hbm, w_ref, packed, vh_ref, vl_ref, sel, vt, ut, sems):
    me, bit = bits(me_ref)
    where = [15 + (me >> 1), 7 + (me >> 2), 3 + (me >> 3), 1 + (me >> 4), 0]
    get_v = pltpu.make_async_copy(vt_hbm, vt, sems.at[0])
    get_u = pltpu.make_async_copy(ut_hbm, ut, sems.at[1])
    picks = [pltpu.make_async_copy(cores_hbm.at[i], sel.at[k], sems.at[2 + k]) for k, i in enumerate(where)]
    for copy in [get_v, get_u, *picks]:
        copy.start()
    get_v.wait()
    get_u.wait()
    vh, vl = split(vt[...])
    vh_ref[...] = vh
    vl_ref[...] = vl
    vh, vl = vh[: 4 * R], vl[: 4 * R]
    uh, ul = split(ut[R:, :])
    w = dot(jnp.concatenate([vh, vl, vh], 1), jnp.concatenate([uh, uh, ul], 1), ((1,), (1,)))
    w_ref[...] = w
    packed[...] = pack(w)
    for copy in picks:
        copy.wait()


def k1(vh, vl, l, yh, yl, lh_ref, ll_ref):
    lh, ll = split(l[...])
    lh_ref[...] = lh
    ll_ref[...] = ll
    yh[...], yl[...] = split(mm3((vh[...], vl[...]), (lh, ll)))


def k2(mine, me_ref, yh, yl, b, g):
    me, bit = bits(me_ref)
    half = g.shape[1]
    at = pl.ds(pl.multiple_of((bit[0] if mine else 1 - bit[0]) * half, half), half)
    g[...] = mm3((yh[...], yl[...]), split(b[:, at]))


def kw(w, w_got, far, far_got, packed, packed_got):
    packed[...] = pack(w[...]) + pack(w_got[...])
    packed_got[...] = far[...] + far_got[...]


def kn(packed, packed_got, out):
    both = packed[:, R:] + packed_got[:, R:]
    out[...] = jnp.concatenate([both[: 3 * R // 2], both[3 * R // 2 :]], 1)


def rows_of(q, bit, own):
    at = bit if own else 1 - bit
    return q[pl.ds(pl.multiple_of(at * R, R), R), :]


def stack(p, first, second, bit):
    p[pl.ds(pl.multiple_of((1 - bit) * R, R), R), :] = first
    p[pl.ds(pl.multiple_of(bit * R, R), R), :] = second


def own_share(core, bit, own, other):
    both = jnp.concatenate([rows_of(core, bit, True), rows_of(core, bit, False)], 0)
    full = mm(jnp.concatenate([own, other], 1), both)
    return jnp.where(bit == 0, full[:, R:], full[:, :R])


def k3(me_ref, g, got, w, w_got, packed, packed_got, sel, m0, m2, m1, m3, p3, q_mine, q_other, p, q, a):
    me, bit = bits(me_ref)
    x = lax.rem(me >> 1, 4)
    c = bit[0]
    share = own_share(sel.at[1], bit[1], packed[:, :R], packed_got[:, :R])
    stack(p, g[4 * R :, :], got[4 * R :, :], c)
    q[...] = mm(sel[0], p[...])
    mine, theirs = rows_of(q, c, True), rows_of(q, c, False)
    q_mine[...] = mine
    q_other[...] = theirs
    wide = jnp.concatenate([w[:, 3 * R :], w_got[:, 3 * R :]], 1)
    left = g[: 4 * R, :] + got[: 4 * R, :] - mm(wide, jnp.concatenate([mine, theirs], 0))
    third = left[3 * R :]
    p3[...] = third
    a[...] = left[: 3 * R] - mm(share, third)
    for d, out in ((2, m2), (1, m1), (3, m3), (0, m0)):
        out[...] = a[:, pl.ds(pl.multiple_of((x ^ d) * 2 * R, 2 * R), 2 * R)]


def unfold(w):
    return jnp.concatenate([w[:, :R], w[:, R:]], 0)


def k4(me_ref, m0, g2, g1, g3, w, w_got, sel, z, q2, p, q):
    me, bit = bits(me_ref)
    own, other = unfold(w), unfold(w_got)
    near = m0[...] + g1[...]
    far = g2[...] + g3[...]
    stack(p, near[2 * R :], far[2 * R :], bit[2])
    q[...] = mm(sel[2], p[...])
    mine, theirs = rows_of(q, bit[2], True), rows_of(q, bit[2], False)
    q2[0] = mine
    q2[1] = theirs
    wide = jnp.concatenate([own[: 2 * R], other[: 2 * R]], 1)
    z[: 2 * R, :] = near[: 2 * R] + far[: 2 * R] - mm(wide, jnp.concatenate([mine, theirs], 0))
    last = own[2 * R :] + other[2 * R :]
    z[2 * R :, :] = jnp.concatenate([last[: R // 2], last[R // 2 :]], 1)


def k5(me_ref, s, got, sel, q1, a0, p, q):
    me, bit = bits(me_ref)
    stack(p, s[R : 2 * R, :], got[R : 2 * R, :], bit[3])
    q[...] = mm(sel[3], p[...])
    mine, theirs = rows_of(q, bit[3], True), rows_of(q, bit[3], False)
    q1[...] = mine
    wide = jnp.concatenate([unfold(s[2 * R :, :]), unfold(got[2 * R :, :])], 1)
    a0[...] = s[:R, :] + got[:R, :] - mm(wide, jnp.concatenate([mine, theirs], 0))


def kr(me_ref, a0, got, sel, q1, q2, r0, r2, r1, r3, p):
    me, bit = bits(me_ref)
    stack(p, a0[...], got[...], bit[4])
    top = mm(rows_of(sel.at[4], bit[4], True), p[...])
    for k, out in ((1, r2), (0, r1), (1, r3), (0, r0)):
        out[:R, :] = top
        out[R : 2 * R, :] = q1[...]
        out[2 * R :, :] = q2[k]


def kq(me_ref, own, got, sel, q, p):
    me, bit = bits(me_ref)
    stack(p, own[...], got[...], bit[1])
    q[...] = mm(rows_of(sel.at[1], bit[1], True), p[...])


def k6(me_ref, r0, r2, r1, r3, q3, q_half):
    me, bit = bits(me_ref)
    x = lax.rem(me >> 1, 4)
    for d, r in ((0, r0), (1, r1), (2, r2), (3, r3)):
        q_half[: 3 * R, pl.ds(pl.multiple_of((x ^ d) * 2 * R, 2 * R), 2 * R)] = r[...]
    q_half[3 * R :, :] = q3[...]


def ku(ut, uh_ref, ul_ref):
    uh_ref[...], ul_ref[...] = split(ut[...].T)


def kl(piece, me_ref, lh, ll, b, uh, ul, q4, x):
    me, bit = bits(me_ref)
    n = x.shape[1]
    at = pl.multiple_of((bit[0] if piece < 2 else 1 - bit[0]) * 2 * n + piece % 2 * n, n)
    bh, bl = split(b[:, pl.ds(at, n)])
    qh, ql = split(q4[:, piece % 2 * n : piece % 2 * n + n])
    right = jnp.concatenate([bh, bh, bl], 0)
    below = jnp.concatenate([qh, qh, ql], 0)
    for k in range(4):
        r = slice(k * 256, k * 256 + 256)
        u4h, u4l = uh[r, 4 * R :], ul[r, 4 * R :]
        x[r, :] = dot(jnp.concatenate([lh[r, :], ll[r, :], lh[r, :]], 1), right) - dot(
            jnp.concatenate([u4h, u4l, u4h], 1), below
        )


def k7(mine, me_ref, xa, xb, uh, ul, q, *rest):
    out, buf, sems = rest[-3:]
    me, bit = bits(me_ref)
    half = q.shape[1]
    at = pl.multiple_of((bit[0] if mine else 1 - bit[0]) * half, half)
    qh, ql = split(q[...])
    right = jnp.concatenate([qh, qh, ql], 0)
    copies = []
    for k in range(4):
        r = slice(k * 256, k * 256 + 256)
        u3h, u3l = uh[r, : 4 * R], ul[r, : 4 * R]
        buf[r, :] = jnp.concatenate([xa[r, :], xb[r, :]], 1) - dot(jnp.concatenate([u3h, u3l, u3h], 1), right)
        copies.append(
            pltpu.make_async_copy(
                buf.at[pl.ds(k * 256, 256)], out.at[pl.ds(k * 256, 256), pl.ds(at, half)], sems.at[k]
            )
        )
        copies[-1].start()
    for copy in copies:
        copy.wait()


def to_other_core(value):
    return lax.ppermute(value, "rows", [(i, i ^ 1) for i in range(32)])


def along(value, shift, d):
    return lax.ppermute(value, "rows", [(i, i ^ (d << shift)) for i in range(32)])


def spread(values, shift):
    return [values[0]] + [along(values[k], shift, d) for k, d in ((1, 2), (2, 1), (3, 3))]


def local(right_side, leaf_inverse, left_factors, right_factors, cores):
    me = lax.axis_index("rows").astype(jnp.int32).reshape(1)
    rows, cols = right_side.shape
    half, eighth = cols // 2, cols // 8
    vt = right_factors.transpose(0, 2, 1).reshape(5 * R, rows)
    ut = left_factors.transpose(0, 2, 1).reshape(5 * R, rows)
    in_hbm = [pltpu.with_memory_space_constraint(v, pltpu.HBM) for v in (vt, ut, cores)]
    tall = shape(5 * R, rows, dtype=BF16)
    square = shape(rows, rows, dtype=BF16)
    after = lax.optimization_barrier

    w, packed, vh, vl, sel = call(
        k0, (me, *in_hbm), [shape(4 * R, 4 * R), shape(3 * R, 2 * R), tall, tall, shape(5, 2 * R, 2 * R)],
        [SM, HB, HB, HB], "couple", 1000, 3 * MIB, 12,
        scratch=[pltpu.VMEM((5 * R, rows), F32)] * 2 + [pltpu.SemaphoreType.DMA((8,))],
    )
    w_got = to_other_core(w)
    far = along(packed, 1, 1)
    yh, yl, lh, ll = call(
        k1, (vh, vl, leaf_inverse), [tall, tall, square, square], [VM] * 3, "project", 1000, 4 * MIB, 20,
    )

    def image(mine, yh_):
        return call(
            lambda *refs: k2(mine, *refs), (me, yh_, yl, right_side), [shape(5 * R, half)], [SM] + [VM] * 3,
            "columns", 10**10 if mine else 1000, 3 * MIB, 12,
        )[0]

    sent = image(False, yh)
    got = to_other_core(sent)
    far = after((far, sent))[0]
    far_got = to_other_core(far)
    g = image(True, after((yh, sent))[0])
    uh, ul = call(
        ku, (after((ut, g))[0],), [shape(rows, 5 * R, dtype=BF16)] * 2, [VM], "turn", 10, 3 * MIB, 8,
    )
    packed, packed_got = call(
        kw, (w, w_got, far, after((far_got, g))[0]), [shape(3 * R, 2 * R)] * 2, [VM] * 4, "chip", 10, MIB, 4,
    )
    *messages, p3, q4_mine, q4_other = call(
        k3, (me, g, got, w, w_got, packed, packed_got, sel),
        [shape(3 * R, eighth)] * 4 + [shape(R, half)] * 3,
        [SM] + [VM] * 7, "level4", 1000, 4 * MIB, 10,
        scratch=[pltpu.VMEM((2 * R, half), F32)] * 2 + [pltpu.VMEM((3 * R, half), F32)],
    )
    (w_next,) = call(
        kn, (packed, after((packed_got, p3))[0]), [shape(3 * R // 2, 2 * R)], [VM] * 2, "chips", 10, MIB, 4,
    )
    w_far = along(w_next, 1, 3)

    def leaf(piece, q4):
        return call(
            lambda *refs: kl(piece, *refs), (me, lh, ll, right_side, uh, ul, q4), [shape(rows, half // 2)],
            [SM] + [VM] * 6, "leaf", 1000, 6 * MIB, 12,
        )[0]

    x0 = leaf(0, q4_mine)
    q4_back = to_other_core(after((q4_other, x0))[0])
    got, x0 = after((spread(messages, 1), x0))
    small = [pltpu.VMEM((2 * R, eighth), F32)]
    z, q2 = call(
        k4, (me, *got, w_next, w_far, sel), [shape(5 * R // 2, eighth), shape(2, R, eighth)],
        [SM] + [VM] * 7, "level2", 1000, MIB, 8, scratch=small * 2,
    )
    got, x1 = after((along(z, 3, 1), leaf(1, after((q4_mine, q2))[0])))
    q1, a0 = call(
        k5, (me, z, got, sel), [shape(R, eighth)] * 2, [SM] + [VM] * 3, "level1", 1000, MIB, 8, scratch=small * 2,
    )
    p3_got = along(after((p3, q1))[0], 1, 1)
    got, x2 = after((along(a0, 3, 3), leaf(2, after((q4_back, q1))[0])))
    back = call(
        kr, (me, a0, got, sel, q1, q2), [shape(3 * R, eighth)] * 4, [SM] + [VM] * 5, "level0", 1000, MIB, 8,
        scratch=small,
    )
    (q3,) = call(
        kq, (me, p3, p3_got, sel), [shape(R, half)], [SM] + [VM] * 3, "level3", 1000, MIB, 8,
        scratch=[pltpu.VMEM((2 * R, half), F32)],
    )
    got, x3, q3 = after((spread(back, 1), leaf(3, after((q4_back, back[0]))[0]), q3))
    (q_half,) = call(k6, (me, *got, q3), [shape(4 * R, half)], [SM] + [VM] * 5, "assemble", 10, MIB, 8)
    q_rest = to_other_core(q_half)

    def finish(mine, xa, xb, q, *so_far):
        return pl.pallas_call(
            lambda *refs: k7(mine, *refs),
            out_shape=shape(rows, cols),
            in_specs=[SM] + [VM] * 5 + [HB] * len(so_far),
            out_specs=HB,
            scratch_shapes=[pltpu.VMEM((rows, half), F32), pltpu.SemaphoreType.DMA((4,))],
            name="finish",
            input_output_aliases={6: 0} if so_far else {},
            cost_estimate=pl.CostEstimate(flops=10**9, bytes_accessed=5 * MIB, transcendentals=0),
            compiler_params=pltpu.CompilerParams(vmem_limit_bytes=10 * MIB),
        )(me, xa, xb, uh, ul, q, *so_far)

    out = finish(True, x0, x1, q_half)
    return finish(False, x2, x3, q_rest, out)


def solution(mesh):
    in_specs = (
        P(("rep", "rows"), None),
        P(("rep", "rows"), None),
        P(None, ("rep", "rows"), None),
        P(None, ("rep", "rows"), None),
        P("rep", None, None),
    )
    out_specs = P(("rep", "rows"), None)
    return jax.shard_map(local, mesh=mesh, in_specs=in_specs, out_specs=out_specs, check_vma=False)
```

```python
import jax
import jax.numpy as jnp
from jax import lax
from jax.experimental import pallas as pl
from jax.experimental.pallas import tpu as pltpu
from jax.sharding import PartitionSpec as P

R = 64
F32, BF16 = jnp.float32, jnp.bfloat16
MIB = 1 << 20


def split(a):
    high = a.astype(BF16)
    return high, (a - high.astype(F32)).astype(BF16)


def dot(a, b, dims=((1,), (0,))):
    return lax.dot_general(a, b, (dims, ((), ())), preferred_element_type=F32)


def mm3(a, b):
    (ah, al), (bh, bl) = a, b
    return dot(jnp.concatenate([ah, al, ah], 1), jnp.concatenate([bh, bh, bl], 0))


def mm(a, b):
    return mm3(split(a), split(b))


def bits(me_ref):
    me = me_ref[0]
    return me, [lax.rem(me >> b, 2) for b in range(5)]


VM = pl.BlockSpec(memory_space=pltpu.VMEM)
SM = pl.BlockSpec(memory_space=pltpu.SMEM)
HB = pl.BlockSpec(memory_space=pltpu.HBM)


def shape(*dims, dtype=F32):
    return jax.ShapeDtypeStruct(dims, dtype)


def call(kernel, ins, outs, specs, name, flops, moved, limit, scratch=(), grid=None, aliases=None):
    out_specs = [VM] * len(outs) if grid is None else grid[1]
    extra = {} if grid is None else dict(grid=grid[0])
    return pl.pallas_call(
        kernel,
        out_shape=tuple(outs),
        in_specs=specs,
        out_specs=tuple(out_specs),
        scratch_shapes=list(scratch),
        name=name,
        input_output_aliases=aliases or {},
        cost_estimate=pl.CostEstimate(flops=flops, bytes_accessed=1000, transcendentals=0),
        compiler_params=pltpu.CompilerParams(vmem_limit_bytes=limit * MIB),
        **extra,
    )(*ins)


def pack(w):
    low = jnp.concatenate([w[: 2 * R, R : 2 * R], w[:R, :R]], 0)
    return jnp.concatenate([w[: 3 * R, 2 * R : 3 * R], low], 1)


def k0(me_ref, vt_hbm, ut_hbm, cores_hbm, w_ref, packed, vh_ref, vl_ref, sel, vt, ut, sems):
    me, bit = bits(me_ref)
    where = [15 + (me >> 1), 7 + (me >> 2), 3 + (me >> 3), 1 + (me >> 4), 1 + ((me >> 4) ^ 1), 0]
    get_v = pltpu.make_async_copy(vt_hbm, vt, sems.at[0])
    get_u = pltpu.make_async_copy(ut_hbm, ut, sems.at[1])
    picks = [pltpu.make_async_copy(cores_hbm.at[i], sel.at[k], sems.at[2 + k]) for k, i in enumerate(where)]
    for copy in [get_v, get_u, *picks]:
        copy.start()
    get_v.wait()
    get_u.wait()
    vh, vl = split(vt[...])
    vh_ref[...] = vh
    vl_ref[...] = vl
    vh, vl = vh[: 4 * R], vl[: 4 * R]
    uh, ul = split(ut[R:, :])
    w = dot(jnp.concatenate([vh, vl, vh], 1), jnp.concatenate([uh, uh, ul], 1), ((1,), (1,)))
    w_ref[...] = w
    packed[...] = pack(w)
    for copy in picks:
        copy.wait()


def k1(vh, vl, l, yh, yl, lh_ref, ll_ref):
    lh, ll = split(l[...])
    lh_ref[...] = lh
    ll_ref[...] = ll
    yh[...], yl[...] = split(mm3((vh[...], vl[...]), (lh, ll)))


def k2(mine, me_ref, yh, yl, b, g):
    me, bit = bits(me_ref)
    half = g.shape[1]
    at = pl.ds(pl.multiple_of((bit[0] if mine else 1 - bit[0]) * half, half), half)
    g[...] = mm3((yh[...], yl[...]), split(b[:, at]))


def rows_of(q, bit, own):
    at = bit if own else 1 - bit
    return q[pl.ds(pl.multiple_of(at * R, R), R), :]


def stack(p, first, second, bit):
    p[pl.ds(pl.multiple_of((1 - bit) * R, R), R), :] = first
    p[pl.ds(pl.multiple_of(bit * R, R), R), :] = second


def own_share(core, bit, own, other):
    both = jnp.concatenate([rows_of(core, bit, True), rows_of(core, bit, False)], 0)
    full = mm(jnp.concatenate([own, other], 1), both)
    return jnp.where(bit == 0, full[:, R:], full[:, :R])


def kw(me_ref, w, w_got, far, far_got, sel, share, w_next):
    me, bit = bits(me_ref)
    own, other = pack(w[...]) + pack(w_got[...]), far[...] + far_got[...]
    share[...] = own_share(sel.at[1], bit[1], own[:, :R], other[:, :R])
    both = own[:, R:] + other[:, R:]
    w_next[...] = jnp.concatenate([both[: 3 * R // 2], both[3 * R // 2 :]], 1)


def k3(me_ref, g, got, w, w_got, share, w_next, sel, m0, m2, m1, m3, p3, q_mine, q_other, p, q, a):
    me, bit = bits(me_ref)
    x = lax.rem(me >> 1, 4)
    c = bit[0]
    stack(p, g[4 * R :, :], got[4 * R :, :], c)
    q[...] = mm(sel[0], p[...])
    mine, theirs = rows_of(q, c, True), rows_of(q, c, False)
    q_mine[...] = mine
    q_other[...] = theirs
    wide = jnp.concatenate([w[:, 3 * R :], w_got[:, 3 * R :]], 1)
    left = g[: 4 * R, :] + got[: 4 * R, :] - mm(wide, jnp.concatenate([mine, theirs], 0))
    third = left[3 * R :]
    p3[...] = third
    a[...] = left[: 3 * R] - mm(share[...], third)
    for d, out in ((2, m2), (1, m1), (3, m3), (0, m0)):
        out[: 3 * R, :] = a[:, pl.ds(pl.multiple_of((x ^ d) * 2 * R, 2 * R), 2 * R)]
    m2[3 * R :, :] = w_next[: 3 * R // 4, :]
    m3[3 * R :, :] = w_next[3 * R // 4 :, :]


def unfold(w):
    return jnp.concatenate([w[:, :R], w[:, R:]], 0)


def k4(me_ref, m0, g2, g1, g3, w, sel, z0, z2, z1, z3, q2, p, q):
    me, bit = bits(me_ref)
    own = unfold(w)
    other = unfold(jnp.concatenate([g2[3 * R :, :], g3[3 * R :, :]], 0))
    near = m0[...] + g1[...]
    far = g2[: 3 * R, :] + g3[: 3 * R, :]
    stack(p, near[2 * R :], far[2 * R :], bit[2])
    q[...] = mm(sel[2], p[...])
    mine, theirs = rows_of(q, bit[2], True), rows_of(q, bit[2], False)
    q2[0] = mine
    q2[1] = theirs
    wide = jnp.concatenate([own[: 2 * R], other[: 2 * R]], 1)
    t = near[: 2 * R] + far[: 2 * R] - mm(wide, jnp.concatenate([mine, theirs], 0))
    last = own[2 * R :] + other[2 * R :]
    last = jnp.concatenate([last[: R // 2], last[R // 2 :]], 1)
    for out in (z2, z1, z3, z0):
        out[: 2 * R, :] = t
        out[2 * R :, :] = last


def k5(me_ref, s0, s2, s1, s3, sel, q2, r0, r2, r1, r3, p, q):
    me, bit = bits(me_ref)
    sums = []
    for k, (a, b) in enumerate(((s0, s1), (s2, s3))):
        stack(p.at[k], a[R : 2 * R, :], b[R : 2 * R, :], bit[3])
        q[k] = mm(sel[3 + k], p[k])
    for k, (a, b) in enumerate(((s0, s1), (s2, s3))):
        both = jnp.concatenate([rows_of(q.at[k], bit[3], True), rows_of(q.at[k], bit[3], False)], 0)
        wide = jnp.concatenate([unfold(a[2 * R :, :]), unfold(b[2 * R :, :])], 1)
        sums.append(a[:R, :] + b[:R, :] - mm(wide, both))
    stack(p.at[2], sums[0], sums[1], bit[4])
    top = mm(rows_of(sel.at[5], bit[4], True), p[2])
    one = rows_of(q.at[0], bit[3], True)
    for k, out in ((1, r2), (0, r1), (1, r3), (0, r0)):
        out[:R, :] = top
        out[R : 2 * R, :] = one
        out[2 * R :, :] = q2[k]


def kq(me_ref, own, got, sel, q, p):
    me, bit = bits(me_ref)
    stack(p, own[...], got[...], bit[1])
    q[...] = mm(rows_of(sel.at[1], bit[1], True), p[...])


def k6(me_ref, r0, r2, r1, r3, q3, q4, q_half):
    me, bit = bits(me_ref)
    x = lax.rem(me >> 1, 4)
    for d, r in ((0, r0), (1, r1), (2, r2), (3, r3)):
        q_half[: 3 * R, pl.ds(pl.multiple_of((x ^ d) * 2 * R, 2 * R), 2 * R)] = r[...]
    q_half[3 * R : 4 * R, :] = q3[...]
    q_half[4 * R :, :] = q4[...]


def ku(ut, uh_ref, ul_ref, u4):
    h, l = split(ut[...].T)
    uh_ref[...] = h[:, : 4 * R]
    ul_ref[...] = l[:, : 4 * R]
    h, l = h[:, 4 * R :], l[:, 4 * R :]
    u4[...] = jnp.concatenate([h, l, h], 1)


def kl(first, me_ref, lh, ll, b, x):
    me, bit = bits(me_ref)
    n = b.shape[1] // 4
    at = pl.multiple_of((bit[0] if first < 2 else 1 - bit[0]) * 2 * n + first % 2 * n, n)
    x[...] = mm3((lh[...], ll[...]), split(b[:, pl.ds(at, x.shape[1])]))


PARTS = 4


def k7(mine, me_ref, xa, xb, uh, ul, u4, q, q4, *rest):
    out, buf, sem = rest[-3:]
    me, bit = bits(me_ref)
    half = q.shape[1]
    at = pl.multiple_of((bit[0] if mine else 1 - bit[0]) * half, half)
    fourth = split(q4[...] if mine else q[4 * R :, :])
    lower = jnp.concatenate([fourth[0], *fourth], 0)
    qh, ql = split(q[: 4 * R, :])
    upper = jnp.concatenate([qh, qh, ql], 0)
    n = buf.shape[0] // PARTS
    copies = []
    for k in range(PARTS):
        r = slice(k * n, k * n + n)
        left = jnp.concatenate([uh[r, :], ul[r, :], uh[r, :]], 1)
        x = xa[r, :] if mine else jnp.concatenate([xa[r, :], xb[r, :]], 1)
        buf[r, :] = x - dot(left, upper) - dot(u4[r, :], lower)
        copies.append(
            pltpu.make_async_copy(buf.at[pl.ds(k * n, n)], out.at[pl.ds(k * n, n), pl.ds(at, half)], sem.at[k])
        )
        copies[-1].start()
    for copy in copies:
        copy.wait()


def to_other_core(value):
    return lax.ppermute(value, "rows", [(i, i ^ 1) for i in range(32)])


def along(value, shift, d):
    return lax.ppermute(value, "rows", [(i, i ^ (d << shift)) for i in range(32)])


def spread(values, shift):
    return [values[0]] + [along(values[k], shift, d) for k, d in ((1, 2), (2, 1), (3, 3))]


def local(right_side, leaf_inverse, left_factors, right_factors, cores):
    me = lax.axis_index("rows").astype(jnp.int32).reshape(1)
    rows, cols = right_side.shape
    half, eighth = cols // 2, cols // 8
    vt = right_factors.transpose(0, 2, 1).reshape(5 * R, rows)
    ut = left_factors.transpose(0, 2, 1).reshape(5 * R, rows)
    in_hbm = [pltpu.with_memory_space_constraint(v, pltpu.HBM) for v in (vt, ut, cores)]
    tall = shape(5 * R, rows, dtype=BF16)
    square = shape(rows, rows, dtype=BF16)
    after = lax.optimization_barrier

    w, packed, vh, vl, sel = call(
        k0, (me, *in_hbm), [shape(4 * R, 4 * R), shape(3 * R, 2 * R), tall, tall, shape(6, 2 * R, 2 * R)],
        [SM, HB, HB, HB], "couple", 1000, 3 * MIB, 12,
        scratch=[pltpu.VMEM((5 * R, rows), F32)] * 2 + [pltpu.SemaphoreType.DMA((8,))],
    )
    w_got = to_other_core(w)
    far = along(packed, 1, 1)
    yh, yl, lh, ll = call(
        k1, (vh, vl, leaf_inverse), [tall, tall, square, square], [VM] * 3, "project", 1000, 4 * MIB, 20,
    )

    def image(mine, yh_):
        return call(
            lambda *refs: k2(mine, *refs), (me, yh_, yl, right_side), [shape(5 * R, half)], [SM] + [VM] * 3,
            "columns", 10**10 if mine else 1000, 3 * MIB, 12,
        )[0]

    sent = image(False, yh)
    got = to_other_core(sent)
    far = after((far, sent))[0]
    far_got = to_other_core(far)
    g = image(True, after((yh, sent))[0])
    far_got, g = after((far_got, g))
    share, w_next = call(
        kw, (me, w, w_got, far, far_got, sel), [shape(3 * R, R), shape(3 * R // 2, 2 * R)], [SM] + [VM] * 5,
        "chip", 10, MIB, 6,
    )
    *messages, p3, q4_mine, q4_other = call(
        k3, (me, g, got, w, w_got, share, w_next, sel),
        [shape(3 * R + k, eighth) for k in (0, 3 * R // 4, 0, 3 * R // 4)] + [shape(R, half)] * 3,
        [SM] + [VM] * 7, "level4", 1000, 4 * MIB, 10,
        scratch=[pltpu.VMEM((2 * R, half), F32)] * 2 + [pltpu.VMEM((3 * R, half), F32)],
    )

    def leaf(first, count, behind):
        return call(
            lambda *refs: kl(first, *refs), (me, after((lh, behind))[0], ll, right_side),
            [shape(rows, count * cols // 4)], [SM] + [VM] * 3, "leaf", 1000, 6 * MIB, 16,
        )[0]

    def turn(behind):
        return call(
            ku, (after((ut, behind))[0],), [shape(rows, k * R, dtype=BF16) for k in (4, 4, 3)], [VM], "turn",
            10, 3 * MIB, 8,
        )

    uh, ul, u4 = turn(q4_mine)
    got, x_mine, uh = after((spread(messages, 1), leaf(0, 2, q4_mine), uh))
    small = [pltpu.VMEM((2 * R, eighth), F32)]
    *z, q2 = call(
        k4, (me, *got, w_next, sel), [shape(5 * R // 2, eighth)] * 4 + [shape(2, R, eighth)],
        [SM] + [VM] * 6, "level2", 1000, MIB, 8, scratch=small * 2,
    )
    got, x2 = after((spread(z, 3), leaf(2, 1, q2)))
    p3_got = along(after((p3, q2))[0], 1, 1)
    back = call(
        k5, (me, *got, sel, q2), [shape(3 * R, eighth)] * 4, [SM] + [VM] * 6, "levels10", 1000, MIB, 8,
        scratch=[pltpu.VMEM((3, 2 * R, eighth), F32), pltpu.VMEM((2, 2 * R, eighth), F32)],
    )
    (q3,) = call(
        kq, (me, p3, p3_got, sel), [shape(R, half)], [SM] + [VM] * 3, "level3", 1000, MIB, 8,
        scratch=[pltpu.VMEM((2 * R, half), F32)],
    )
    got, x3, q3 = after((spread(back, 1), leaf(3, 1, back[0]), q3))
    (q_half,) = call(
        k6, (me, *got, q3, q4_other), [shape(5 * R, half)], [SM] + [VM] * 6, "assemble", 10, MIB, 8,
    )
    q_rest = to_other_core(q_half)

    def finish(mine, xa, xb, q, *so_far):
        return pl.pallas_call(
            lambda *refs: k7(mine, *refs),
            out_shape=shape(rows, cols),
            in_specs=[SM] + [VM] * 7 + [HB] * len(so_far),
            out_specs=HB,
            scratch_shapes=[pltpu.VMEM((rows, half), F32), pltpu.SemaphoreType.DMA((PARTS,))],
            name="finish",
            input_output_aliases={8: 0} if so_far else {},
            cost_estimate=pl.CostEstimate(flops=10**9, bytes_accessed=5 * MIB, transcendentals=0),
            compiler_params=pltpu.CompilerParams(vmem_limit_bytes=12 * MIB),
        )(me, xa, xb, uh, ul, u4, q, q4_mine, *so_far)

    out = finish(True, x_mine, x_mine, q_half)
    return finish(False, x2, x3, q_rest, out)


def solution(mesh):
    in_specs = (
        P(("rep", "rows"), None),
        P(("rep", "rows"), None),
        P(None, ("rep", "rows"), None),
        P(None, ("rep", "rows"), None),
        P("rep", None, None),
    )
    out_specs = P(("rep", "rows"), None)
    return jax.shard_map(local, mesh=mesh, in_specs=in_specs, out_specs=out_specs, check_vma=False)
```

```python
import jax
import jax.numpy as jnp
from jax import lax
from jax.experimental import pallas as pl
from jax.experimental.pallas import tpu as pltpu
from jax.sharding import PartitionSpec as P

R = 64
F32, BF16 = jnp.float32, jnp.bfloat16
MIB = 1 << 20


def split(a):
    high = a.astype(BF16)
    return high, (a - high.astype(F32)).astype(BF16)


def dot(a, b, dims=((1,), (0,))):
    return lax.dot_general(a, b, (dims, ((), ())), preferred_element_type=F32)


def mm3(a, b):
    (ah, al), (bh, bl) = a, b
    return dot(jnp.concatenate([ah, al, ah], 1), jnp.concatenate([bh, bh, bl], 0))


def mm(a, b):
    return mm3(split(a), split(b))


def bits(me_ref):
    me = me_ref[0]
    return me, [lax.rem(me >> b, 2) for b in range(5)]


VM = pl.BlockSpec(memory_space=pltpu.VMEM)
SM = pl.BlockSpec(memory_space=pltpu.SMEM)
HB = pl.BlockSpec(memory_space=pltpu.HBM)


def shape(*dims, dtype=F32):
    return jax.ShapeDtypeStruct(dims, dtype)


def call(kernel, ins, outs, specs, name, flops, moved, limit, scratch=(), grid=None, aliases=None):
    out_specs = [VM] * len(outs) if grid is None else grid[1]
    extra = {} if grid is None else dict(grid=grid[0])
    return pl.pallas_call(
        kernel,
        out_shape=tuple(outs),
        in_specs=specs,
        out_specs=tuple(out_specs),
        scratch_shapes=list(scratch),
        name=name,
        input_output_aliases=aliases or {},
        cost_estimate=pl.CostEstimate(flops=flops, bytes_accessed=1000, transcendentals=0),
        compiler_params=pltpu.CompilerParams(vmem_limit_bytes=limit * MIB),
        **extra,
    )(*ins)


def pack(w):
    low = jnp.concatenate([w[: 2 * R, R : 2 * R], w[:R, :R]], 0)
    return jnp.concatenate([w[: 3 * R, 2 * R : 3 * R], low], 1)


def k0(me_ref, vt_hbm, ut_hbm, cores_hbm, w_ref, packed, vh_ref, vl_ref, sel, vt, ut, sems):
    me, bit = bits(me_ref)
    where = [15 + (me >> 1), 7 + (me >> 2), 3 + (me >> 3), 1 + (me >> 4), 1 + ((me >> 4) ^ 1), 0]
    get_v = pltpu.make_async_copy(vt_hbm, vt, sems.at[0])
    get_u = pltpu.make_async_copy(ut_hbm, ut, sems.at[1])
    picks = [pltpu.make_async_copy(cores_hbm.at[i], sel.at[k], sems.at[2 + k]) for k, i in enumerate(where)]
    for copy in [get_v, get_u, *picks]:
        copy.start()
    get_v.wait()
    get_u.wait()
    vh, vl = split(vt[...])
    vh_ref[...] = vh
    vl_ref[...] = vl
    vh, vl = vh[: 4 * R], vl[: 4 * R]
    uh, ul = split(ut[R:, :])
    w = dot(jnp.concatenate([vh, vl, vh], 1), jnp.concatenate([uh, uh, ul], 1), ((1,), (1,)))
    w_ref[...] = w
    packed[...] = pack(w)
    for copy in picks:
        copy.wait()


def k1(vh, vl, l, yh, yl, lh_ref, ll_ref):
    lh, ll = split(l[...])
    lh_ref[...] = lh
    ll_ref[...] = ll
    yh[...], yl[...] = split(mm3((vh[...], vl[...]), (lh, ll)))


def k2(mine, me_ref, yh, yl, b, g):
    me, bit = bits(me_ref)
    half = g.shape[1]
    at = pl.ds(pl.multiple_of((bit[0] if mine else 1 - bit[0]) * half, half), half)
    g[...] = mm3((yh[...], yl[...]), split(b[:, at]))


def rows_of(q, bit, own):
    at = bit if own else 1 - bit
    return q[pl.ds(pl.multiple_of(at * R, R), R), :]


def stack(p, first, second, bit):
    p[pl.ds(pl.multiple_of((1 - bit) * R, R), R), :] = first
    p[pl.ds(pl.multiple_of(bit * R, R), R), :] = second


def own_share(core, bit, own, other):
    both = jnp.concatenate([rows_of(core, bit, True), rows_of(core, bit, False)], 0)
    full = mm(jnp.concatenate([own, other], 1), both)
    return jnp.where(bit == 0, full[:, R:], full[:, :R])


def kw(w, w_got, far, far_got, packed, packed_got):
    packed[...] = pack(w[...]) + pack(w_got[...])
    packed_got[...] = far[...] + far_got[...]


def k3(me_ref, g, got, w, w_got, packed, packed_got, sel, m0, m2, m1, m3, p3, q_mine, q_other, w_next, p, q, a):
    me, bit = bits(me_ref)
    x = lax.rem(me >> 1, 4)
    c = bit[0]
    share = own_share(sel.at[1], bit[1], packed[:, :R], packed_got[:, :R])
    stack(p, g[4 * R :, :], got[4 * R :, :], c)
    q[...] = mm(sel[0], p[...])
    mine, theirs = rows_of(q, c, True), rows_of(q, c, False)
    q_mine[...] = mine
    q_other[...] = theirs
    wide = jnp.concatenate([w[:, 3 * R :], w_got[:, 3 * R :]], 1)
    left = g[: 4 * R, :] + got[: 4 * R, :] - mm(wide, jnp.concatenate([mine, theirs], 0))
    third = left[3 * R :]
    p3[...] = third
    a[...] = left[: 3 * R] - mm(share, third)
    for d, out in ((2, m2), (1, m1), (3, m3), (0, m0)):
        out[: 3 * R, :] = a[:, pl.ds(pl.multiple_of((x ^ d) * 2 * R, 2 * R), 2 * R)]
    both = packed[:, R:] + packed_got[:, R:]
    both = jnp.concatenate([both[: 3 * R // 2], both[3 * R // 2 :]], 1)
    w_next[...] = both
    m2[3 * R :, :] = both[: 3 * R // 4]
    m3[3 * R :, :] = both[3 * R // 4 :]


def unfold(w):
    return jnp.concatenate([w[:, :R], w[:, R:]], 0)


def k4(me_ref, m0, g2, g1, g3, w, sel, z0, z2, z1, z3, q2, p, q):
    me, bit = bits(me_ref)
    own = unfold(w)
    other = unfold(jnp.concatenate([g2[3 * R :, :], g3[3 * R :, :]], 0))
    near = m0[...] + g1[...]
    far = g2[: 3 * R, :] + g3[: 3 * R, :]
    stack(p, near[2 * R :], far[2 * R :], bit[2])
    q[...] = mm(sel[2], p[...])
    mine, theirs = rows_of(q, bit[2], True), rows_of(q, bit[2], False)
    q2[0] = mine
    q2[1] = theirs
    wide = jnp.concatenate([own[: 2 * R], other[: 2 * R]], 1)
    t = near[: 2 * R] + far[: 2 * R] - mm(wide, jnp.concatenate([mine, theirs], 0))
    last = own[2 * R :] + other[2 * R :]
    last = jnp.concatenate([last[: R // 2], last[R // 2 :]], 1)
    for out in (z2, z1, z3, z0):
        out[: 2 * R, :] = t
        out[2 * R :, :] = last


def k5(me_ref, s0, s2, s1, s3, sel, q2, r0, r2, r1, r3, p, q):
    me, bit = bits(me_ref)
    sums = []
    for k, (a, b) in enumerate(((s0, s1), (s2, s3))):
        stack(p.at[k], a[R : 2 * R, :], b[R : 2 * R, :], bit[3])
        q[k] = mm(sel[3 + k], p[k])
    for k, (a, b) in enumerate(((s0, s1), (s2, s3))):
        both = jnp.concatenate([rows_of(q.at[k], bit[3], True), rows_of(q.at[k], bit[3], False)], 0)
        wide = jnp.concatenate([unfold(a[2 * R :, :]), unfold(b[2 * R :, :])], 1)
        sums.append(a[:R, :] + b[:R, :] - mm(wide, both))
    stack(p.at[2], sums[0], sums[1], bit[4])
    top = mm(rows_of(sel.at[5], bit[4], True), p[2])
    one = rows_of(q.at[0], bit[3], True)
    for k, out in ((1, r2), (0, r1), (1, r3), (0, r0)):
        out[:R, :] = top
        out[R : 2 * R, :] = one
        out[2 * R :, :] = q2[k]


def kq(me_ref, own, got, sel, q, p):
    me, bit = bits(me_ref)
    stack(p, own[...], got[...], bit[1])
    q[...] = mm(rows_of(sel.at[1], bit[1], True), p[...])


def k6(me_ref, r0, r2, r1, r3, q3, q_half):
    me, bit = bits(me_ref)
    x = lax.rem(me >> 1, 4)
    for d, r in ((0, r0), (1, r1), (2, r2), (3, r3)):
        q_half[: 3 * R, pl.ds(pl.multiple_of((x ^ d) * 2 * R, 2 * R), 2 * R)] = r[...]
    q_half[3 * R :, :] = q3[...]


def ku(ut, uh_ref, ul_ref, u4):
    h, l = split(ut[...].T)
    uh_ref[...] = h[:, : 4 * R]
    ul_ref[...] = l[:, : 4 * R]
    h, l = h[:, 4 * R :], l[:, 4 * R :]
    u4[...] = jnp.concatenate([h, l, h], 1)


def below(q):
    h, l = split(q)
    return jnp.concatenate([h, h, l], 0)


def kl(first, me_ref, lh, ll, b, u4, q4, x):
    me, bit = bits(me_ref)
    n = b.shape[1] // 4
    within = first % 2 * n
    at = pl.multiple_of((bit[0] if first < 2 else 1 - bit[0]) * 2 * n + within, n)
    leaf = mm3((lh[...], ll[...]), split(b[:, pl.ds(at, x.shape[1])]))
    x[...] = leaf - dot(u4[...], below(q4[:, within : within + x.shape[1]]))


PARTS = 4


def k7(mine, me_ref, xa, xb, uh, ul, q, *rest):
    out, buf, sem = rest[-3:]
    me, bit = bits(me_ref)
    half = q.shape[1]
    at = pl.multiple_of((bit[0] if mine else 1 - bit[0]) * half, half)
    right = below(q[...])
    n = buf.shape[0] // PARTS
    copies = []
    for k in range(PARTS):
        r = slice(k * n, k * n + n)
        left = jnp.concatenate([uh[r, :], ul[r, :], uh[r, :]], 1)
        x = xa[r, :] if mine else jnp.concatenate([xa[r, :], xb[r, :]], 1)
        buf[r, :] = x - dot(left, right)
        copies.append(
            pltpu.make_async_copy(buf.at[pl.ds(k * n, n)], out.at[pl.ds(k * n, n), pl.ds(at, half)], sem.at[k])
        )
        copies[-1].start()
    for copy in copies:
        copy.wait()


def to_other_core(value):
    return lax.ppermute(value, "rows", [(i, i ^ 1) for i in range(32)])


def along(value, shift, d):
    return lax.ppermute(value, "rows", [(i, i ^ (d << shift)) for i in range(32)])


def spread(values, shift):
    return [values[0]] + [along(values[k], shift, d) for k, d in ((1, 2), (2, 1), (3, 3))]


def local(right_side, leaf_inverse, left_factors, right_factors, cores):
    me = lax.axis_index("rows").astype(jnp.int32).reshape(1)
    rows, cols = right_side.shape
    half, eighth = cols // 2, cols // 8
    vt = right_factors.transpose(0, 2, 1).reshape(5 * R, rows)
    ut = left_factors.transpose(0, 2, 1).reshape(5 * R, rows)
    in_hbm = [pltpu.with_memory_space_constraint(v, pltpu.HBM) for v in (vt, ut, cores)]
    tall = shape(5 * R, rows, dtype=BF16)
    square = shape(rows, rows, dtype=BF16)
    after = lax.optimization_barrier

    w, packed, vh, vl, sel = call(
        k0, (me, *in_hbm), [shape(4 * R, 4 * R), shape(3 * R, 2 * R), tall, tall, shape(6, 2 * R, 2 * R)],
        [SM, HB, HB, HB], "couple", 1000, 3 * MIB, 12,
        scratch=[pltpu.VMEM((5 * R, rows), F32)] * 2 + [pltpu.SemaphoreType.DMA((8,))],
    )
    w_got = to_other_core(w)
    far = along(packed, 1, 1)
    yh, yl, lh, ll = call(
        k1, (vh, vl, leaf_inverse), [tall, tall, square, square], [VM] * 3, "project", 1000, 4 * MIB, 20,
    )

    def image(mine, yh_):
        return call(
            lambda *refs: k2(mine, *refs), (me, yh_, yl, right_side), [shape(5 * R, half)], [SM] + [VM] * 3,
            "columns", 10**10 if mine else 1000, 3 * MIB, 12,
        )[0]

    sent = image(False, yh)
    got = to_other_core(sent)
    far = after((far, sent))[0]
    far_got = to_other_core(far)
    g = image(True, after((yh, sent))[0])
    far_got, g = after((far_got, g))
    packed, packed_got = call(
        kw, (w, w_got, far, far_got), [shape(3 * R, 2 * R)] * 2, [VM] * 4, "chip", 10, MIB, 4,
    )
    *messages, p3, q4_mine, q4_other, w_next = call(
        k3, (me, g, got, w, w_got, packed, packed_got, sel),
        [shape(3 * R + k, eighth) for k in (0, 3 * R // 4, 0, 3 * R // 4)] + [shape(R, half)] * 3
        + [shape(3 * R // 2, 2 * R)],
        [SM] + [VM] * 7, "level4", 1000, 4 * MIB, 10,
        scratch=[pltpu.VMEM((2 * R, half), F32)] * 2 + [pltpu.VMEM((3 * R, half), F32)],
    )

    def leaf(first, count, q4, behind):
        return call(
            lambda *refs: kl(first, *refs), (me, after((lh, behind))[0], ll, right_side, u4, q4),
            [shape(rows, count * cols // 4)], [SM] + [VM] * 5, "leaf", 1000, 6 * MIB, 16,
        )[0]

    def turn(behind):
        return call(
            ku, (after((ut, behind))[0],), [shape(rows, k * R, dtype=BF16) for k in (4, 4, 3)], [VM], "turn",
            10, 3 * MIB, 8,
        )

    uh, ul, u4 = turn(q4_mine)
    x_mine = leaf(0, 2, q4_mine, q4_mine)
    q4_back = to_other_core(after((q4_other, x_mine))[0])
    got, x_mine = after((spread(messages, 1), x_mine))
    small = [pltpu.VMEM((2 * R, eighth), F32)]
    *z, q2 = call(
        k4, (me, *got, w_next, sel), [shape(5 * R // 2, eighth)] * 4 + [shape(2, R, eighth)],
        [SM] + [VM] * 6, "level2", 1000, MIB, 8, scratch=small * 2,
    )
    got, x2 = after((spread(z, 3), leaf(2, 1, q4_back, q2)))
    p3_got = along(after((p3, q2))[0], 1, 1)
    back = call(
        k5, (me, *got, sel, q2), [shape(3 * R, eighth)] * 4, [SM] + [VM] * 6, "levels10", 1000, MIB, 8,
        scratch=[pltpu.VMEM((3, 2 * R, eighth), F32), pltpu.VMEM((2, 2 * R, eighth), F32)],
    )
    (q3,) = call(
        kq, (me, p3, p3_got, sel), [shape(R, half)], [SM] + [VM] * 3, "level3", 1000, MIB, 8,
        scratch=[pltpu.VMEM((2 * R, half), F32)],
    )
    got, x3, q3 = after((spread(back, 1), leaf(3, 1, q4_back, back[0]), q3))
    (q_half,) = call(
        k6, (me, *got, q3), [shape(4 * R, half)], [SM] + [VM] * 5, "assemble", 10, MIB, 8,
    )
    q_rest = to_other_core(q_half)

    def finish(mine, xa, xb, q, *so_far):
        return pl.pallas_call(
            lambda *refs: k7(mine, *refs),
            out_shape=shape(rows, cols),
            in_specs=[SM] + [VM] * 5 + [HB] * len(so_far),
            out_specs=HB,
            scratch_shapes=[pltpu.VMEM((rows, half), F32), pltpu.SemaphoreType.DMA((PARTS,))],
            name="finish",
            input_output_aliases={6: 0} if so_far else {},
            cost_estimate=pl.CostEstimate(flops=10**9, bytes_accessed=5 * MIB, transcendentals=0),
            compiler_params=pltpu.CompilerParams(vmem_limit_bytes=12 * MIB),
        )(me, xa, xb, uh, ul, q, *so_far)

    out = finish(True, x_mine, x_mine, q_half)
    return finish(False, x2, x3, q_rest, out)


def solution(mesh):
    in_specs = (
        P(("rep", "rows"), None),
        P(("rep", "rows"), None),
        P(None, ("rep", "rows"), None),
        P(None, ("rep", "rows"), None),
        P("rep", None, None),
    )
    out_specs = P(("rep", "rows"), None)
    return jax.shard_map(local, mesh=mesh, in_specs=in_specs, out_specs=out_specs, check_vma=False)
```

```python
import jax
import jax.numpy as jnp
from jax import lax
from jax.experimental import pallas as pl
from jax.experimental.pallas import tpu as pltpu
from jax.sharding import PartitionSpec as P

R = 64
F32, BF16 = jnp.float32, jnp.bfloat16
MIB = 1 << 20


def split(a):
    high = a.astype(BF16)
    return high, (a - high.astype(F32)).astype(BF16)


def dot(a, b, dims=((1,), (0,))):
    return lax.dot_general(a, b, (dims, ((), ())), preferred_element_type=F32)


def mm3(a, b):
    (ah, al), (bh, bl) = a, b
    return dot(jnp.concatenate([ah, al, ah], 1), jnp.concatenate([bh, bh, bl], 0))


def mm(a, b):
    return mm3(split(a), split(b))


def bits(me_ref):
    me = me_ref[0]
    return me, [lax.rem(me >> b, 2) for b in range(5)]


VM = pl.BlockSpec(memory_space=pltpu.VMEM)
SM = pl.BlockSpec(memory_space=pltpu.SMEM)
HB = pl.BlockSpec(memory_space=pltpu.HBM)


def shape(*dims, dtype=F32):
    return jax.ShapeDtypeStruct(dims, dtype)


def call(kernel, ins, outs, specs, name, flops, moved, limit, scratch=(), grid=None, aliases=None):
    out_specs = [VM] * len(outs) if grid is None else grid[1]
    extra = {} if grid is None else dict(grid=grid[0])
    return pl.pallas_call(
        kernel,
        out_shape=tuple(outs),
        in_specs=specs,
        out_specs=tuple(out_specs),
        scratch_shapes=list(scratch),
        name=name,
        input_output_aliases=aliases or {},
        cost_estimate=pl.CostEstimate(flops=flops, bytes_accessed=1000, transcendentals=0),
        compiler_params=pltpu.CompilerParams(vmem_limit_bytes=limit * MIB),
        **extra,
    )(*ins)


def pack(w):
    low = jnp.concatenate([w[: 2 * R, R : 2 * R], w[:R, :R]], 0)
    return jnp.concatenate([w[: 3 * R, 2 * R : 3 * R], low], 1)


def k0(me_ref, vt_hbm, ut_hbm, cores_hbm, w_ref, packed, vh_ref, vl_ref, sel, vt, ut, sems):
    me, bit = bits(me_ref)
    where = [15 + (me >> 1), 7 + (me >> 2), 3 + (me >> 3), 1 + (me >> 4), 1 + ((me >> 4) ^ 1), 0]
    get_v = pltpu.make_async_copy(vt_hbm, vt, sems.at[0])
    get_u = pltpu.make_async_copy(ut_hbm, ut, sems.at[1])
    picks = [pltpu.make_async_copy(cores_hbm.at[i], sel.at[k], sems.at[2 + k]) for k, i in enumerate(where)]
    for copy in [get_v, get_u, *picks]:
        copy.start()
    get_v.wait()
    get_u.wait()
    vh, vl = split(vt[...])
    vh_ref[...] = vh
    vl_ref[...] = vl
    vh, vl = vh[: 4 * R], vl[: 4 * R]
    uh, ul = split(ut[R:, :])
    w = dot(jnp.concatenate([vh, vl, vh], 1), jnp.concatenate([uh, uh, ul], 1), ((1,), (1,)))
    w_ref[...] = w
    packed[...] = pack(w)
    for copy in picks:
        copy.wait()


def k1(vh, vl, l, yh, yl, lh_ref, ll_ref):
    lh, ll = split(l[...])
    lh_ref[...] = lh
    ll_ref[...] = ll
    yh[...], yl[...] = split(mm3((vh[...], vl[...]), (lh, ll)))


def k2(mine, me_ref, yh, yl, b, g):
    me, bit = bits(me_ref)
    half = g.shape[1]
    at = pl.ds(pl.multiple_of((bit[0] if mine else 1 - bit[0]) * half, half), half)
    g[...] = mm3((yh[...], yl[...]), split(b[:, at]))


def rows_of(q, bit, own):
    at = bit if own else 1 - bit
    return q[pl.ds(pl.multiple_of(at * R, R), R), :]


def stack(p, first, second, bit):
    p[pl.ds(pl.multiple_of((1 - bit) * R, R), R), :] = first
    p[pl.ds(pl.multiple_of(bit * R, R), R), :] = second


def own_share(core, bit, own, other):
    both = jnp.concatenate([rows_of(core, bit, True), rows_of(core, bit, False)], 0)
    full = mm(jnp.concatenate([own, other], 1), both)
    return jnp.where(bit == 0, full[:, R:], full[:, :R])


def kw(w, w_got, far, far_got, packed, packed_got):
    packed[...] = pack(w[...]) + pack(w_got[...])
    packed_got[...] = far[...] + far_got[...]


def k3(me_ref, g, got, w, w_got, packed, packed_got, sel, m0, m2, m1, m3, p3, q_mine, q_other, w_next, p, q, a):
    me, bit = bits(me_ref)
    x = lax.rem(me >> 1, 4)
    c = bit[0]
    share = own_share(sel.at[1], bit[1], packed[:, :R], packed_got[:, :R])
    stack(p, g[4 * R :, :], got[4 * R :, :], c)
    q[...] = mm(sel[0], p[...])
    mine, theirs = rows_of(q, c, True), rows_of(q, c, False)
    q_mine[...] = mine
    q_other[...] = theirs
    wide = jnp.concatenate([w[:, 3 * R :], w_got[:, 3 * R :]], 1)
    left = g[: 4 * R, :] + got[: 4 * R, :] - mm(wide, jnp.concatenate([mine, theirs], 0))
    third = left[3 * R :]
    p3[...] = third
    a[...] = left[: 3 * R] - mm(share, third)
    for d, out in ((2, m2), (1, m1), (3, m3), (0, m0)):
        out[: 3 * R, :] = a[:, pl.ds(pl.multiple_of((x ^ d) * 2 * R, 2 * R), 2 * R)]
    both = packed[:, R:] + packed_got[:, R:]
    both = jnp.concatenate([both[: 3 * R // 2], both[3 * R // 2 :]], 1)
    w_next[...] = both
    m3[3 * R :, :] = both


def unfold(w):
    return jnp.concatenate([w[:, :R], w[:, R:]], 0)


def k4(me_ref, m0, g2, g1, g3, w, sel, z0, z2, z1, z3, q2, p, q):
    me, bit = bits(me_ref)
    own = unfold(w)
    other = unfold(g3[3 * R :, :])
    near = m0[...] + g1[...]
    far = g2[...] + g3[: 3 * R, :]
    stack(p, near[2 * R :], far[2 * R :], bit[2])
    q[...] = mm(sel[2], p[...])
    mine, theirs = rows_of(q, bit[2], True), rows_of(q, bit[2], False)
    q2[0] = mine
    q2[1] = theirs
    wide = jnp.concatenate([own[: 2 * R], other[: 2 * R]], 1)
    t = near[: 2 * R] + far[: 2 * R] - mm(wide, jnp.concatenate([mine, theirs], 0))
    last = own[2 * R :] + other[2 * R :]
    last = jnp.concatenate([last[: R // 2], last[R // 2 :]], 1)
    for out in (z2, z1, z3, z0):
        out[: 2 * R, :] = t
        out[2 * R :, :] = last


def k5(me_ref, s0, s2, s1, s3, sel, q2, r0, r2, r1, r3, p, q):
    me, bit = bits(me_ref)
    sums = []
    for k, (a, b) in enumerate(((s0, s1), (s2, s3))):
        stack(p.at[k], a[R : 2 * R, :], b[R : 2 * R, :], bit[3])
        q[k] = mm(sel[3 + k], p[k])
    for k, (a, b) in enumerate(((s0, s1), (s2, s3))):
        both = jnp.concatenate([rows_of(q.at[k], bit[3], True), rows_of(q.at[k], bit[3], False)], 0)
        wide = jnp.concatenate([unfold(a[2 * R :, :]), unfold(b[2 * R :, :])], 1)
        sums.append(a[:R, :] + b[:R, :] - mm(wide, both))
    stack(p.at[2], sums[0], sums[1], bit[4])
    top = mm(rows_of(sel.at[5], bit[4], True), p[2])
    one = rows_of(q.at[0], bit[3], True)
    for k, out in ((1, r2), (0, r1), (1, r3), (0, r0)):
        out[:R, :] = top
        out[R : 2 * R, :] = one
        out[2 * R :, :] = q2[k]


def kq(me_ref, own, got, sel, q, p):
    me, bit = bits(me_ref)
    stack(p, own[...], got[...], bit[1])
    q[...] = mm(rows_of(sel.at[1], bit[1], True), p[...])


def k6(me_ref, r0, r2, r1, r3, q3, q_half):
    me, bit = bits(me_ref)
    x = lax.rem(me >> 1, 4)
    for d, r in ((0, r0), (1, r1), (2, r2), (3, r3)):
        q_half[: 3 * R, pl.ds(pl.multiple_of((x ^ d) * 2 * R, 2 * R), 2 * R)] = r[...]
    q_half[3 * R :, :] = q3[...]


def ku(ut, uh_ref, ul_ref, u4):
    h, l = split(ut[...].T)
    uh_ref[...] = h[:, : 4 * R]
    ul_ref[...] = l[:, : 4 * R]
    h, l = h[:, 4 * R :], l[:, 4 * R :]
    u4[...] = jnp.concatenate([h, l, h], 1)


def below(q):
    h, l = split(q)
    return jnp.concatenate([h, h, l], 0)


def kl(first, me_ref, lh, ll, b, u4, q4, x):
    me, bit = bits(me_ref)
    n = b.shape[1] // 4
    within = first % 2 * n
    at = pl.multiple_of((bit[0] if first < 2 else 1 - bit[0]) * 2 * n + within, n)
    leaf = mm3((lh[...], ll[...]), split(b[:, pl.ds(at, x.shape[1])]))
    x[...] = leaf - dot(u4[...], below(q4[:, within : within + x.shape[1]]))


PARTS = 4


def k7(mine, me_ref, xa, xb, uh, ul, q, *rest):
    out, buf, sem = rest[-3:]
    me, bit = bits(me_ref)
    half = q.shape[1]
    at = pl.multiple_of((bit[0] if mine else 1 - bit[0]) * half, half)
    right = below(q[...])
    n = buf.shape[0] // PARTS
    copies = []
    for k in range(PARTS):
        r = slice(k * n, k * n + n)
        left = jnp.concatenate([uh[r, :], ul[r, :], uh[r, :]], 1)
        x = xa[r, :] if mine else jnp.concatenate([xa[r, :], xb[r, :]], 1)
        buf[r, :] = x - dot(left, right)
        copies.append(
            pltpu.make_async_copy(buf.at[pl.ds(k * n, n)], out.at[pl.ds(k * n, n), pl.ds(at, half)], sem.at[k])
        )
        copies[-1].start()
    for copy in copies:
        copy.wait()


def to_other_core(value):
    return lax.ppermute(value, "rows", [(i, i ^ 1) for i in range(32)])


def along(value, shift, d):
    return lax.ppermute(value, "rows", [(i, i ^ (d << shift)) for i in range(32)])


def spread(values, shift):
    return [values[0]] + [along(values[k], shift, d) for k, d in ((1, 2), (2, 1), (3, 3))]


def local(right_side, leaf_inverse, left_factors, right_factors, cores):
    me = lax.axis_index("rows").astype(jnp.int32).reshape(1)
    rows, cols = right_side.shape
    half, eighth = cols // 2, cols // 8
    vt = right_factors.transpose(0, 2, 1).reshape(5 * R, rows)
    ut = left_factors.transpose(0, 2, 1).reshape(5 * R, rows)
    in_hbm = [pltpu.with_memory_space_constraint(v, pltpu.HBM) for v in (vt, ut, cores)]
    tall = shape(5 * R, rows, dtype=BF16)
    square = shape(rows, rows, dtype=BF16)
    after = lax.optimization_barrier

    w, packed, vh, vl, sel = call(
        k0, (me, *in_hbm), [shape(4 * R, 4 * R), shape(3 * R, 2 * R), tall, tall, shape(6, 2 * R, 2 * R)],
        [SM, HB, HB, HB], "couple", 1000, 3 * MIB, 12,
        scratch=[pltpu.VMEM((5 * R, rows), F32)] * 2 + [pltpu.SemaphoreType.DMA((8,))],
    )
    w_got = to_other_core(w)
    far = along(packed, 1, 1)
    yh, yl, lh, ll = call(
        k1, (vh, vl, leaf_inverse), [tall, tall, square, square], [VM] * 3, "project", 1000, 4 * MIB, 20,
    )

    def image(mine, yh_):
        return call(
            lambda *refs: k2(mine, *refs), (me, yh_, yl, right_side), [shape(5 * R, half)], [SM] + [VM] * 3,
            "columns", 10**10 if mine else 1000, 3 * MIB, 12,
        )[0]

    sent = image(False, yh)
    got = to_other_core(sent)
    far = after((far, sent))[0]
    far_got = to_other_core(far)
    g = image(True, after((yh, sent))[0])
    far_got, g = after((far_got, g))
    packed, packed_got = call(
        kw, (w, w_got, far, far_got), [shape(3 * R, 2 * R)] * 2, [VM] * 4, "chip", 10, MIB, 4,
    )
    *messages, p3, q4_mine, q4_other, w_next = call(
        k3, (me, g, got, w, w_got, packed, packed_got, sel),
        [shape(3 * R + k, eighth) for k in (0, 0, 0, 3 * R // 2)] + [shape(R, half)] * 3
        + [shape(3 * R // 2, 2 * R)],
        [SM] + [VM] * 7, "level4", 1000, 4 * MIB, 10,
        scratch=[pltpu.VMEM((2 * R, half), F32)] * 2 + [pltpu.VMEM((3 * R, half), F32)],
    )

    def leaf(first, count, q4, behind):
        return call(
            lambda *refs: kl(first, *refs), (me, after((lh, behind))[0], ll, right_side, u4, q4),
            [shape(rows, count * cols // 4)], [SM] + [VM] * 5, "leaf", 1000, 6 * MIB, 16,
        )[0]

    def turn(behind):
        return call(
            ku, (after((ut, behind))[0],), [shape(rows, k * R, dtype=BF16) for k in (4, 4, 3)], [VM], "turn",
            10, 3 * MIB, 8,
        )

    uh, ul, u4 = turn(q4_mine)
    x_mine = leaf(0, 2, q4_mine, q4_mine)
    q4_back = to_other_core(after((q4_other, x_mine))[0])
    got, x_mine = after((spread(messages, 1), x_mine))
    small = [pltpu.VMEM((2 * R, eighth), F32)]
    *z, q2 = call(
        k4, (me, *got, w_next, sel), [shape(5 * R // 2, eighth)] * 4 + [shape(2, R, eighth)],
        [SM] + [VM] * 6, "level2", 1000, MIB, 8, scratch=small * 2,
    )
    got, x2 = after((spread(z, 3), leaf(2, 1, q4_back, q2)))
    p3_got = along(after((p3, q2))[0], 1, 1)
    back = call(
        k5, (me, *got, sel, q2), [shape(3 * R, eighth)] * 4, [SM] + [VM] * 6, "levels10", 1000, MIB, 8,
        scratch=[pltpu.VMEM((3, 2 * R, eighth), F32), pltpu.VMEM((2, 2 * R, eighth), F32)],
    )
    (q3,) = call(
        kq, (me, p3, p3_got, sel), [shape(R, half)], [SM] + [VM] * 3, "level3", 1000, MIB, 8,
        scratch=[pltpu.VMEM((2 * R, half), F32)],
    )
    got, x3, q3 = after((spread(back, 1), leaf(3, 1, q4_back, back[0]), q3))
    (q_half,) = call(
        k6, (me, *got, q3), [shape(4 * R, half)], [SM] + [VM] * 5, "assemble", 10, MIB, 8,
    )
    q_rest = to_other_core(q_half)

    def finish(mine, xa, xb, q, *so_far):
        return pl.pallas_call(
            lambda *refs: k7(mine, *refs),
            out_shape=shape(rows, cols),
            in_specs=[SM] + [VM] * 5 + [HB] * len(so_far),
            out_specs=HB,
            scratch_shapes=[pltpu.VMEM((rows, half), F32), pltpu.SemaphoreType.DMA((PARTS,))],
            name="finish",
            input_output_aliases={6: 0} if so_far else {},
            cost_estimate=pl.CostEstimate(flops=10**9, bytes_accessed=5 * MIB, transcendentals=0),
            compiler_params=pltpu.CompilerParams(vmem_limit_bytes=12 * MIB),
        )(me, xa, xb, uh, ul, q, *so_far)

    out = finish(True, x_mine, x_mine, q_half)
    return finish(False, x2, x3, q_rest, out)


def solution(mesh):
    in_specs = (
        P(("rep", "rows"), None),
        P(("rep", "rows"), None),
        P(None, ("rep", "rows"), None),
        P(None, ("rep", "rows"), None),
        P("rep", None, None),
    )
    out_specs = P(("rep", "rows"), None)
    return jax.shard_map(local, mesh=mesh, in_specs=in_specs, out_specs=out_specs, check_vma=False)
```

```python
import jax
import jax.numpy as jnp
from jax import lax
from jax.experimental import pallas as pl
from jax.experimental.pallas import tpu as pltpu
from jax.sharding import PartitionSpec as P

R = 64
F32, BF16 = jnp.float32, jnp.bfloat16
MIB = 1 << 20


def split(a):
    high = a.astype(BF16)
    return high, (a - high.astype(F32)).astype(BF16)


def dot(a, b, dims=((1,), (0,))):
    return lax.dot_general(a, b, (dims, ((), ())), preferred_element_type=F32)


def mm3(a, b):
    (ah, al), (bh, bl) = a, b
    return dot(jnp.concatenate([ah, al, ah], 1), jnp.concatenate([bh, bh, bl], 0))


def mm(a, b):
    return mm3(split(a), split(b))


def bits(me_ref):
    me = me_ref[0]
    return me, [lax.rem(me >> b, 2) for b in range(5)]


VM = pl.BlockSpec(memory_space=pltpu.VMEM)
SM = pl.BlockSpec(memory_space=pltpu.SMEM)
HB = pl.BlockSpec(memory_space=pltpu.HBM)


def shape(*dims, dtype=F32):
    return jax.ShapeDtypeStruct(dims, dtype)


def call(kernel, ins, outs, specs, name, flops, moved, limit, scratch=(), grid=None, aliases=None):
    out_specs = [VM] * len(outs) if grid is None else grid[1]
    extra = {} if grid is None else dict(grid=grid[0])
    return pl.pallas_call(
        kernel,
        out_shape=tuple(outs),
        in_specs=specs,
        out_specs=tuple(out_specs),
        scratch_shapes=list(scratch),
        name=name,
        input_output_aliases=aliases or {},
        cost_estimate=pl.CostEstimate(flops=flops, bytes_accessed=1000, transcendentals=0),
        compiler_params=pltpu.CompilerParams(vmem_limit_bytes=limit * MIB),
        **extra,
    )(*ins)


def pack(w):
    low = jnp.concatenate([w[: 2 * R, R : 2 * R], w[:R, :R]], 0)
    return jnp.concatenate([w[: 3 * R, 2 * R : 3 * R], low], 1)


def k0(me_ref, vt_hbm, ut_hbm, cores_hbm, w_ref, packed, vh_ref, vl_ref, sel, vt, ut, sems):
    me, bit = bits(me_ref)
    where = [15 + (me >> 1), 7 + (me >> 2), 3 + (me >> 3), 1 + (me >> 4), 1 + ((me >> 4) ^ 1), 0]
    get_v = pltpu.make_async_copy(vt_hbm, vt, sems.at[0])
    get_u = pltpu.make_async_copy(ut_hbm, ut, sems.at[1])
    picks = [pltpu.make_async_copy(cores_hbm.at[i], sel.at[k], sems.at[2 + k]) for k, i in enumerate(where)]
    for copy in [get_v, get_u, *picks]:
        copy.start()
    get_v.wait()
    get_u.wait()
    vh, vl = split(vt[...])
    vh_ref[...] = vh
    vl_ref[...] = vl
    vh, vl = vh[: 4 * R], vl[: 4 * R]
    uh, ul = split(ut[R:, :])
    w = dot(jnp.concatenate([vh, vl, vh], 1), jnp.concatenate([uh, uh, ul], 1), ((1,), (1,)))
    w_ref[...] = w
    packed[...] = pack(w)
    for copy in picks:
        copy.wait()


def k1(vh, vl, l, yh, yl, lh_ref, ll_ref):
    lh, ll = split(l[...])
    lh_ref[...] = lh
    ll_ref[...] = ll
    yh[...], yl[...] = split(mm3((vh[...], vl[...]), (lh, ll)))


def k2(mine, me_ref, yh, yl, b, g):
    me, bit = bits(me_ref)
    half = g.shape[1]
    at = pl.ds(pl.multiple_of((bit[0] if mine else 1 - bit[0]) * half, half), half)
    g[...] = mm3((yh[...], yl[...]), split(b[:, at]))


def rows_of(q, bit, own):
    at = bit if own else 1 - bit
    return q[pl.ds(pl.multiple_of(at * R, R), R), :]


def stack(p, first, second, bit):
    p[pl.ds(pl.multiple_of((1 - bit) * R, R), R), :] = first
    p[pl.ds(pl.multiple_of(bit * R, R), R), :] = second


def own_share(core, bit, own, other):
    both = jnp.concatenate([rows_of(core, bit, True), rows_of(core, bit, False)], 0)
    full = mm(jnp.concatenate([own, other], 1), both)
    return jnp.where(bit == 0, full[:, R:], full[:, :R])


def kw(w, w_got, far, far_got, packed, packed_got):
    packed[...] = pack(w[...]) + pack(w_got[...])
    packed_got[...] = far[...] + far_got[...]


def k3(me_ref, g, got, w, w_got, packed, packed_got, sel, m0, m2, m1, m3, p3, q_mine, q_other, w_next, p, q, a):
    me, bit = bits(me_ref)
    x = lax.rem(me >> 1, 4)
    c = bit[0]
    share = own_share(sel.at[1], bit[1], packed[:, :R], packed_got[:, :R])
    stack(p, g[4 * R :, :], got[4 * R :, :], c)
    q[...] = mm(sel[0], p[...])
    mine, theirs = rows_of(q, c, True), rows_of(q, c, False)
    q_mine[...] = mine
    q_other[...] = theirs
    wide = jnp.concatenate([w[:, 3 * R :], w_got[:, 3 * R :]], 1)
    left = g[: 4 * R, :] + got[: 4 * R, :] - mm(wide, jnp.concatenate([mine, theirs], 0))
    third = left[3 * R :]
    p3[...] = third
    a[...] = left[: 3 * R] - mm(share, third)
    for d, out in ((2, m2), (1, m1), (3, m3), (0, m0)):
        out[: 3 * R, :] = a[:, pl.ds(pl.multiple_of((x ^ d) * 2 * R, 2 * R), 2 * R)]
    both = packed[:, R:] + packed_got[:, R:]
    both = jnp.concatenate([both[: 3 * R // 2], both[3 * R // 2 :]], 1)
    w_next[...] = both
    m3[3 * R :, :] = both


def unfold(w):
    return jnp.concatenate([w[:, :R], w[:, R:]], 0)


def k4(me_ref, m0, g2, g1, g3, w, sel, z0, z3, z2, z1, q2, p, q):
    me, bit = bits(me_ref)
    own = unfold(w)
    other = unfold(g3[3 * R :, :])
    near = m0[...] + g1[...]
    far = g2[...] + g3[: 3 * R, :]
    stack(p, near[2 * R :], far[2 * R :], bit[2])
    q[...] = mm(sel[2], p[...])
    mine, theirs = rows_of(q, bit[2], True), rows_of(q, bit[2], False)
    q2[0] = mine
    q2[1] = theirs
    wide = jnp.concatenate([own[: 2 * R], other[: 2 * R]], 1)
    t = near[: 2 * R] + far[: 2 * R] - mm(wide, jnp.concatenate([mine, theirs], 0))
    last = own[2 * R :] + other[2 * R :]
    last = jnp.concatenate([last[: R // 2], last[R // 2 :]], 1)
    for out in (z2, z1, z3, z0):
        out[: 2 * R, :] = t
        out[2 * R :, :] = last


def k5(me_ref, s0, s3, s2, s1, sel, q2, r0, r3, r2, r1, p, q):
    me, bit = bits(me_ref)
    sums = []
    for k, (a, b) in enumerate(((s0, s1), (s2, s3))):
        stack(p.at[k], a[R : 2 * R, :], b[R : 2 * R, :], bit[3])
        q[k] = mm(sel[3 + k], p[k])
    for k, (a, b) in enumerate(((s0, s1), (s2, s3))):
        both = jnp.concatenate([rows_of(q.at[k], bit[3], True), rows_of(q.at[k], bit[3], False)], 0)
        wide = jnp.concatenate([unfold(a[2 * R :, :]), unfold(b[2 * R :, :])], 1)
        sums.append(a[:R, :] + b[:R, :] - mm(wide, both))
    stack(p.at[2], sums[0], sums[1], bit[4])
    top = mm(rows_of(sel.at[5], bit[4], True), p[2])
    one = rows_of(q.at[0], bit[3], True)
    for k, out in ((1, r2), (0, r1), (1, r3), (0, r0)):
        out[:R, :] = top
        out[R : 2 * R, :] = one
        out[2 * R :, :] = q2[k]


def kq(me_ref, own, got, sel, q, p):
    me, bit = bits(me_ref)
    stack(p, own[...], got[...], bit[1])
    q[...] = mm(rows_of(sel.at[1], bit[1], True), p[...])


def k6(me_ref, r0, r3, r2, r1, q3, q_half):
    me, bit = bits(me_ref)
    x = lax.rem(me >> 1, 4)
    for d, r in ((0, r0), (1, r1), (2, r2), (3, r3)):
        q_half[: 3 * R, pl.ds(pl.multiple_of((x ^ d) * 2 * R, 2 * R), 2 * R)] = r[...]
    q_half[3 * R :, :] = q3[...]


def ku(ut, uh_ref, ul_ref, u4):
    h, l = split(ut[...].T)
    uh_ref[...] = h[:, : 4 * R]
    ul_ref[...] = l[:, : 4 * R]
    h, l = h[:, 4 * R :], l[:, 4 * R :]
    u4[...] = jnp.concatenate([h, l, h], 1)


def below(q):
    h, l = split(q)
    return jnp.concatenate([h, h, l], 0)


def kl(first, me_ref, lh, ll, b, u4, q4, x):
    me, bit = bits(me_ref)
    n = b.shape[1] // 4
    within = first % 2 * n
    at = pl.multiple_of((bit[0] if first < 2 else 1 - bit[0]) * 2 * n + within, n)
    leaf = mm3((lh[...], ll[...]), split(b[:, pl.ds(at, x.shape[1])]))
    x[...] = leaf - dot(u4[...], below(q4[:, within : within + x.shape[1]]))


PARTS = 4


def k7(mine, me_ref, xa, xb, uh, ul, q, *rest):
    out, buf, sem = rest[-3:]
    me, bit = bits(me_ref)
    half = q.shape[1]
    at = pl.multiple_of((bit[0] if mine else 1 - bit[0]) * half, half)
    right = below(q[...])
    n = buf.shape[0] // PARTS
    copies = []
    for k in range(PARTS):
        r = slice(k * n, k * n + n)
        left = jnp.concatenate([uh[r, :], ul[r, :], uh[r, :]], 1)
        x = xa[r, :] if mine else jnp.concatenate([xa[r, :], xb[r, :]], 1)
        buf[r, :] = x - dot(left, right)
        copies.append(
            pltpu.make_async_copy(buf.at[pl.ds(k * n, n)], out.at[pl.ds(k * n, n), pl.ds(at, half)], sem.at[k])
        )
        copies[-1].start()
    for copy in copies:
        copy.wait()


def to_other_core(value):
    return lax.ppermute(value, "rows", [(i, i ^ 1) for i in range(32)])


def along(value, shift, d):
    return lax.ppermute(value, "rows", [(i, i ^ (d << shift)) for i in range(32)])


def spread(values, shift, order=(2, 1, 3)):
    return [values[0]] + [along(values[k + 1], shift, d) for k, d in enumerate(order)]


def local(right_side, leaf_inverse, left_factors, right_factors, cores):
    me = lax.axis_index("rows").astype(jnp.int32).reshape(1)
    rows, cols = right_side.shape
    half, eighth = cols // 2, cols // 8
    vt = right_factors.transpose(0, 2, 1).reshape(5 * R, rows)
    ut = left_factors.transpose(0, 2, 1).reshape(5 * R, rows)
    in_hbm = [pltpu.with_memory_space_constraint(v, pltpu.HBM) for v in (vt, ut, cores)]
    tall = shape(5 * R, rows, dtype=BF16)
    square = shape(rows, rows, dtype=BF16)
    after = lax.optimization_barrier

    w, packed, vh, vl, sel = call(
        k0, (me, *in_hbm), [shape(4 * R, 4 * R), shape(3 * R, 2 * R), tall, tall, shape(6, 2 * R, 2 * R)],
        [SM, HB, HB, HB], "couple", 1000, 3 * MIB, 12,
        scratch=[pltpu.VMEM((5 * R, rows), F32)] * 2 + [pltpu.SemaphoreType.DMA((8,))],
    )
    w_got = to_other_core(w)
    far = along(packed, 1, 1)
    yh, yl, lh, ll = call(
        k1, (vh, vl, leaf_inverse), [tall, tall, square, square], [VM] * 3, "project", 1000, 4 * MIB, 20,
    )

    def image(mine, yh_):
        return call(
            lambda *refs: k2(mine, *refs), (me, yh_, yl, right_side), [shape(5 * R, half)], [SM] + [VM] * 3,
            "columns", 10**10 if mine else 1000, 3 * MIB, 12,
        )[0]

    sent = image(False, yh)
    got = to_other_core(sent)
    far = after((far, sent))[0]
    far_got = to_other_core(far)
    g = image(True, after((yh, sent))[0])
    far_got, g = after((far_got, g))
    packed, packed_got = call(
        kw, (w, w_got, far, far_got), [shape(3 * R, 2 * R)] * 2, [VM] * 4, "chip", 10, MIB, 4,
    )
    *messages, p3, q4_mine, q4_other, w_next = call(
        k3, (me, g, got, w, w_got, packed, packed_got, sel),
        [shape(3 * R + k, eighth) for k in (0, 0, 0, 3 * R // 2)] + [shape(R, half)] * 3
        + [shape(3 * R // 2, 2 * R)],
        [SM] + [VM] * 7, "level4", 1000, 4 * MIB, 10,
        scratch=[pltpu.VMEM((2 * R, half), F32)] * 2 + [pltpu.VMEM((3 * R, half), F32)],
    )

    def leaf(first, count, q4, behind):
        return call(
            lambda *refs: kl(first, *refs), (me, after((lh, behind))[0], ll, right_side, u4, q4),
            [shape(rows, count * cols // 4)], [SM] + [VM] * 5, "leaf", 1000, 6 * MIB, 16,
        )[0]

    def turn(behind):
        return call(
            ku, (after((ut, behind))[0],), [shape(rows, k * R, dtype=BF16) for k in (4, 4, 3)], [VM], "turn",
            10, 3 * MIB, 8,
        )

    uh, ul, u4 = turn(q4_mine)
    x_mine = leaf(0, 2, q4_mine, q4_mine)
    q4_back = to_other_core(after((q4_other, x_mine))[0])
    got, x_mine = after((spread(messages, 1), x_mine))
    small = [pltpu.VMEM((2 * R, eighth), F32)]
    *z, q2 = call(
        k4, (me, *got, w_next, sel), [shape(5 * R // 2, eighth)] * 4 + [shape(2, R, eighth)],
        [SM] + [VM] * 6, "level2", 1000, MIB, 8, scratch=small * 2,
    )
    got, x2 = after((spread(z, 3, (3, 2, 1)), leaf(2, 1, q4_back, q2)))
    p3_got = along(after((p3, q2))[0], 1, 1)
    back = call(
        k5, (me, *got, sel, q2), [shape(3 * R, eighth)] * 4, [SM] + [VM] * 6, "levels10", 1000, MIB, 8,
        scratch=[pltpu.VMEM((3, 2 * R, eighth), F32), pltpu.VMEM((2, 2 * R, eighth), F32)],
    )
    (q3,) = call(
        kq, (me, p3, p3_got, sel), [shape(R, half)], [SM] + [VM] * 3, "level3", 1000, MIB, 8,
        scratch=[pltpu.VMEM((2 * R, half), F32)],
    )
    got, x3, q3 = after((spread(back, 1, (3, 2, 1)), leaf(3, 1, q4_back, back[0]), q3))
    (q_half,) = call(
        k6, (me, *got, q3), [shape(4 * R, half)], [SM] + [VM] * 5, "assemble", 10, MIB, 8,
    )
    q_rest = to_other_core(q_half)

    def finish(mine, xa, xb, q, *so_far):
        return pl.pallas_call(
            lambda *refs: k7(mine, *refs),
            out_shape=shape(rows, cols),
            in_specs=[SM] + [VM] * 5 + [HB] * len(so_far),
            out_specs=HB,
            scratch_shapes=[pltpu.VMEM((rows, half), F32), pltpu.SemaphoreType.DMA((PARTS,))],
            name="finish",
            input_output_aliases={6: 0} if so_far else {},
            cost_estimate=pl.CostEstimate(flops=10**9, bytes_accessed=5 * MIB, transcendentals=0),
            compiler_params=pltpu.CompilerParams(vmem_limit_bytes=12 * MIB),
        )(me, xa, xb, uh, ul, q, *so_far)

    out = finish(True, x_mine, x_mine, q_half)
    return finish(False, x2, x3, q_rest, out)


def solution(mesh):
    in_specs = (
        P(("rep", "rows"), None),
        P(("rep", "rows"), None),
        P(None, ("rep", "rows"), None),
        P(None, ("rep", "rows"), None),
        P("rep", None, None),
    )
    out_specs = P(("rep", "rows"), None)
    return jax.shard_map(local, mesh=mesh, in_specs=in_specs, out_specs=out_specs, check_vma=False)
```
